128 devices in a mesh: frames: 32 (over z, y, core), points: 4 (over x).
Axes of the slice: x: 4, y: 4, z: 4, core: 2. Of those that a mesh axis runs over, the one named last changes fastest.
Arguments:
- obs_count: int32 [512], P(('frames', 'points')), may hold values from 128 to 2048, as said below
- obs_point: int32 [1048576], P(('frames', 'points')), may hold values from 0 to 1023
- obs_frame: int32 [1048576], P(('frames', 'points')), may hold values from 0 to 255
- jac_cam: float32 [2, 6, 1048576], P(None, None, ('frames', 'points')), may hold values from -4 to 4
- jac_point: float32 [2, 24, 1048576], P(None, None, ('frames', 'points')), may hold values from -1.25 to 1.25
- residual: float32 [2, 1048576], P(None, ('frames', 'points')), may hold values from -38 to 38
- point_inv: float32 [24, 24, 131072], P(None, None, ('frames', 'points')), may hold values from -1 to 2
- band: float32 [127, 6, 6, 8192], P(None, None, None, 'frames'), may hold values from -1 to 8, as said below
- edge_weight: float32 [8192], P('frames'), may hold values from 0.5 to 5
- precond: float32 [6, 6, 8192], P(None, None, 'frames'), may hold values from -1 to 1, as said below
Outputs:
- camera_step: float32 [6, 8192], P(None, 'frames')
- point_step: float32 [24, 131072], P(None, ('frames', 'points'))
The draws below stay inside these ranges and needn't reach their ends.
Inputs may be any that keep to these rules, and one draw needn't show every extreme that they name: `obs_count`: multiples of 128; in one frame block, chosen anew for each draw, every device of that block uses all 2048 slots toward one same owner block; other counts vary. `band`: a symmetric positive definite matrix over all frames: the block at offset k of frame f is the transpose of the block at offset 127 - 1 - k of frame f + k - 63. `precond`: each frame's block is symmetric positive definite.
All inputs are finite; a program needn't handle non-finite values.
Results may differ from the reference program's by a relative error of at most 0.0001.
Values sent between devices are 32-bit elements; how exact they have to be, the bound alone decides.
No kernel may reach another device: no remote copies, remote signals or barrier semaphores. Data moves between devices by JAX's collectives and lax.ppermute only.
A program may use at most 128 MiB of HBM per device.

```python
import math
import jax
import jax.numpy as jnp
from jax import lax

CP = 6
Q = 24
BAND = 64
BANDW = 127
TILE = 128
ITERS = 2
FR_DEV = 256
PT_DEV = 1024
CAP = 2048
FRAMES = 8192
POINTS = 131072
OBS_DEV = 8192
OBS = 1048576
N_FRAMES = 32
N_POINTS = 4


def draw_obs_count(key, part):
    entry_count = N_FRAMES * N_POINTS * N_POINTS
    key_one, key_two, key_three = jax.random.split(jax.random.fold_in(key, 11), 3)
    tile_counts = jax.random.randint(key_one, (entry_count,), 1, CAP // TILE + 1) * TILE
    full_row = jax.random.randint(key_two, (), 0, N_FRAMES)
    target = jax.random.randint(key_three, (), 0, N_POINTS)
    entry_order = jnp.arange(entry_count)
    owner_block = entry_order % N_POINTS
    frame_block = entry_order // N_POINTS // N_POINTS
    filled = (frame_block == full_row) & (owner_block == target)
    return jnp.where(filled, CAP, tile_counts).astype(jnp.int32)


def draw_residual(key, part):
    key_one, key_two = jax.random.split(jax.random.fold_in(key, 12), 2)
    slot_order = jnp.arange(OBS)
    frame_block = slot_order // OBS_DEV // N_POINTS
    ramp_scale = 1.0 + 2.0 * frame_block.astype(jnp.float32) / max(N_FRAMES - 1, 1)
    spread = jnp.exp(jax.random.uniform(key_two, (OBS,), jnp.float32, -1.15, 1.15))
    base_draw = jnp.clip(jax.random.normal(key_one, (2, OBS), jnp.float32), -4.0, 4.0)
    return (base_draw * ramp_scale * spread).astype(jnp.float32)


def symmetric_blocks(key, size, count, off_bound, low, high):
    key_one, key_two = jax.random.split(key, 2)
    raw_draw = jax.random.uniform(key_one, (size, size, count), jnp.float32, -off_bound, off_bound)
    symmetric = 0.5 * (raw_draw + jnp.transpose(raw_draw, (1, 0, 2)))
    diagonal = jax.random.uniform(key_two, (size, count), jnp.float32, low, high)
    identity = jnp.eye(size, dtype=jnp.float32)[:, :, None]
    return symmetric * (1.0 - identity) + identity * diagonal[None, :, :]


def draw_precond(key, part):
    return symmetric_blocks(jax.random.fold_in(key, 13), CP, FRAMES, 0.012, 0.08, 0.25)


def draw_point_inv(key, part):
    return symmetric_blocks(jax.random.fold_in(key, 14), Q, POINTS, 0.4 / Q, 0.5, 1.5)


def draw_band(key, part):
    key_one, key_two = jax.random.split(jax.random.fold_in(key, 15), 2)
    reach_back = BAND - 1
    off_bound = 0.025
    raw_draw = jax.random.uniform(key_one, (BANDW, CP, CP, FRAMES), jnp.float32, -off_bound, off_bound)
    flipped = jnp.transpose(raw_draw, (0, 2, 1, 3))
    offsets = jnp.arange(BANDW)
    source_frame = jnp.clip(jnp.arange(FRAMES)[None, :] + offsets[:, None] - reach_back, 0, FRAMES - 1)
    mirrored = flipped[(BANDW - 1 - offsets)[:, None, None, None], jnp.arange(CP)[None, :, None, None], jnp.arange(CP)[None, None, :, None], source_frame[:, None, None, :]]
    lower_part = (offsets < reach_back)[:, None, None, None]
    combined = jnp.where(lower_part, mirrored, raw_draw)
    center = symmetric_blocks(key_two, CP, FRAMES, off_bound, 4.0, 8.0)
    return combined.at[reach_back].set(center).astype(jnp.float32)


def with_ends(drawn, key, smallest, high):
    extent = drawn.shape
    spot = [jax.random.randint(jax.random.fold_in(key, axis), (), 0, extent[axis]) for axis in range(len(extent))]
    drawn = drawn.at[tuple(spot)].set(smallest)
    longest = extent.index(max(extent))
    spot[longest] = (spot[longest] + 1) % extent[longest]
    return drawn.at[tuple(spot)].set(high)


def level_of(key, shape, cuts, smallest, largest):
    def one(axis_at, shards_of):
        heights = jax.random.uniform(jax.random.fold_in(jax.random.fold_in(key, 6), axis_at), (shards_of,), jnp.float32, smallest / len(cuts), largest / len(cuts))
        return jnp.repeat(jnp.exp(heights), shape[axis_at] // shards_of).reshape((-1,) + (1,) * (len(shape) - axis_at - 1))

    level = one(*cuts[0])
    for cut in cuts[1:]:
        level = level * one(*cut)
    return level


def normal_values(key, shape, width, reach, cuts=(), kind=jnp.bfloat16):
    entries = width * jax.random.normal(key, shape, jnp.float32)
    if cuts:
        entries = entries * level_of(key, shape, cuts, -0.22, 0.18)
    return jnp.clip(entries, -reach, reach).astype(kind)


def setup_inputs(seed: int = 0) -> dict:
    splits = jax.random.split(jax.random.key(seed), 11)
    obs_count = draw_obs_count(jax.random.fold_in(splits[10], 71), 0)
    obs_point = with_ends(jax.random.randint(splits[1], (OBS,), 0, PT_DEV), jax.random.fold_in(splits[1], 1), 0, PT_DEV - 1).astype(jnp.int32)
    obs_frame = with_ends(jax.random.randint(splits[2], (OBS,), 0, FR_DEV), jax.random.fold_in(splits[2], 1), 0, FR_DEV - 1).astype(jnp.int32)
    jac_cam = normal_values(splits[3], (2, CP, OBS), 0.25, 4.0, ((2, 128),), jnp.float32)
    jac_point = normal_values(splits[4], (2, Q, OBS), Q ** -0.5, 1.25, ((2, 128),), jnp.float32)
    residual = draw_residual(jax.random.fold_in(splits[10], 71), 0)
    point_inv = draw_point_inv(jax.random.fold_in(splits[10], 71), 0)
    band = draw_band(jax.random.fold_in(splits[10], 71), 0)
    edge_weight = jnp.clip(jnp.exp(math.log(5.0) - 2.3025851 * jax.random.uniform(splits[8], (FRAMES,), jnp.float32) ** level_of(splits[8], (FRAMES,), ((0, 32),), -0.2, 0.2)), 0.5, 5.0)
    precond = draw_precond(jax.random.fold_in(splits[10], 71), 0)
    return dict(obs_count=obs_count, obs_point=obs_point, obs_frame=obs_frame, jac_cam=jac_cam, jac_point=jac_point, residual=residual, point_inv=point_inv, band=band, edge_weight=edge_weight, precond=precond)


HIGHEST = lax.Precision.HIGHEST


def apply_operator(field_in, band, edge_weight):
    reach_back = BAND - 1
    padded = jnp.pad(field_in, ((0, 0), (reach_back, reach_back)))
    window_idx = jnp.arange(FRAMES)[None, :] + jnp.arange(BANDW)[:, None]
    window = padded[:, window_idx]
    banded = jnp.einsum("kijf,jkf->if", band, window, precision=HIGHEST)
    edge_here = edge_weight * (jnp.arange(FRAMES) < FRAMES - 1).astype(edge_weight.dtype)
    edge_prev = jnp.concatenate([jnp.zeros((1,), edge_weight.dtype), edge_here[:-1]])
    before = padded[:, reach_back - 1:reach_back - 1 + FRAMES]
    after_frame = padded[:, reach_back + 1:reach_back + 1 + FRAMES]
    return banded + edge_prev * (field_in - before) + edge_here * (field_in - after_frame)


def precondition(precond, vector_in):
    return jnp.einsum("ijf,jf->if", precond, vector_in, precision=HIGHEST)


def point_sum(jac_point, pairs, used_slot, point_ids):
    grad_terms = jnp.einsum("aqo,ao->qo", jac_point, pairs, precision=HIGHEST) * used_slot
    return jax.ops.segment_sum(grad_terms.T, point_ids, num_segments=POINTS).T


def reference(obs_count, obs_point, obs_frame, jac_cam, jac_point, residual, point_inv, band, edge_weight, precond):
    slot_order = jnp.arange(OBS, dtype=jnp.int32)
    device = slot_order // OBS_DEV
    slot_in = slot_order % OBS_DEV
    owner_block = slot_in // CAP
    within = slot_in % CAP
    frame_block = device // N_POINTS
    used_slot = (within < obs_count[device * N_POINTS + owner_block]).astype(residual.dtype)
    point_ids = ((frame_block * N_POINTS + owner_block) * PT_DEV + obs_point).astype(jnp.int32)
    frame_ids = (frame_block * FR_DEV + obs_frame).astype(jnp.int32)

    point_grad = point_sum(jac_point, residual, used_slot, point_ids)
    point_solved = jnp.einsum("ijp,jp->ip", point_inv, point_grad, precision=HIGHEST)
    seen_values = point_solved[:, point_ids]
    remain = residual - jnp.einsum("aqo,qo->ao", jac_point, seen_values, precision=HIGHEST)
    cam_terms = jnp.einsum("aco,ao->co", jac_cam, remain, precision=HIGHEST) * used_slot
    rhs = jax.ops.segment_sum(cam_terms.T, frame_ids, num_segments=FRAMES).T

    camera_step = jnp.zeros_like(rhs)
    remainder = rhs
    scaled = precondition(precond, remainder)
    direction = scaled
    inner_now = jnp.sum(remainder * scaled)
    for step_index in range(ITERS):
        image_now = apply_operator(direction, band, edge_weight)
        step_size = inner_now / jnp.sum(direction * image_now)
        camera_step = camera_step + step_size * direction
        remainder = remainder - step_size * image_now
        if step_index + 1 < ITERS:
            scaled = precondition(precond, remainder)
            inner_next = jnp.sum(remainder * scaled)
            direction = scaled + (inner_next / inner_now) * direction
            inner_now = inner_next

    shifted_res = residual - jnp.einsum("aco,co->ao", jac_cam, camera_step[:, frame_ids], precision=HIGHEST)
    update_grad = point_sum(jac_point, shifted_res, used_slot, point_ids)
    point_step = jnp.einsum("ijp,jp->ip", point_inv, update_grad, precision=HIGHEST)
    return camera_step, point_step
```

```python
import functools

import jax
import jax.numpy as jnp
from jax import lax
from jax.experimental import pallas as pl
from jax.experimental.pallas import tpu as pltpu
from jax.sharding import PartitionSpec as P

F32 = jnp.float32
BF16 = jnp.bfloat16
CP = 6
Q = 24
BANDW = 127
REACH = 63
FR = 256
PT = 1024
CAP = 2048
GROUPS = 4
LO = 256
HI = PT // LO


def halves(x):
    lead = x.astype(BF16).astype(F32)
    return jnp.concatenate([lead, x - lead], axis=0).astype(BF16)


def one_hot(row, rows):
    n = row.shape[1]
    index = lax.broadcasted_iota(jnp.int32, (rows, 128), 0).astype(F32).astype(BF16)
    row = row.astype(BF16)
    cols = []
    for c in range(n // 128):
        here = jnp.broadcast_to(row[:, c * 128 : (c + 1) * 128], (rows, 128))
        cols.append(jnp.where(index == here, jnp.ones_like(index), jnp.zeros_like(index)))
    return jnp.concatenate(cols, axis=1)


def split_ids(ids):
    hi = lax.shift_right_logical(ids, 8)
    lo = lax.bitwise_and(ids, LO - 1)
    return hi.astype(F32), lo.astype(F32)


def used_row(count):
    lane = lax.broadcasted_iota(jnp.int32, (1, CAP), 1)
    return (lane < count).astype(F32)


def scatter_points(terms, ids):
    n = terms.shape[0]
    hi, lo = split_ids(ids)
    parts = halves(terms)
    table = one_hot(lo, LO)
    rows = []
    for h in range(HI):
        mask = jnp.broadcast_to((hi == h).astype(F32), (2 * n, CAP)).astype(BF16)
        rows.append(parts * mask)
    sums = lax.dot_general(
        jnp.concatenate(rows, axis=0), table, (((1,), (1,)), ((), ())), preferred_element_type=F32
    )
    out = []
    for h in range(HI):
        block = sums[h * 2 * n : (h + 1) * 2 * n]
        out.append(block[:n] + block[n:])
    return jnp.concatenate(out, axis=1)


def gather_points(values, ids):
    n = values.shape[0]
    hi, lo = split_ids(ids)
    parts = halves(values)
    table = one_hot(lo, LO)
    stacked = jnp.concatenate([parts[:, h * LO : (h + 1) * LO] for h in range(HI)], axis=0)
    got = lax.dot_general(stacked, table, (((1,), (0,)), ((), ())), preferred_element_type=F32)
    total = None
    for h in range(HI):
        block = got[h * 2 * n : (h + 1) * 2 * n]
        term = (block[:n] + block[n:]) * (hi == h).astype(F32)
        total = term if total is None else total + term
    return total


def grad_kernel(me_ref, count_ref, ids_ref, res_ref, jp_ref, *outs):
    k = pl.program_id(0)
    b = lax.rem(me_ref[0] + GROUPS - 1 - k, GROUPS)
    used = used_row(count_ref[b])
    res = res_ref[...] * used
    terms = jp_ref[0] * res[0:1] + jp_ref[1] * res[1:2]
    sums = scatter_points(terms, ids_ref[...])
    for j in range(GROUPS):

        @pl.when(k == j)
        def _():
            outs[j][...] = sums


def solve_kernel(a_ref, b_ref, c_ref, d_ref, inv_ref, out_ref):
    grad = a_ref[...] + b_ref[...] + c_ref[...] + d_ref[...]
    out_ref[...] = jnp.sum(inv_ref[...] * grad[None], axis=1)


def rhs_kernel(me_ref, count_ref, pid_ref, fid_ref, res_ref, jp_ref, jc_ref, *rest):
    solved, out_ref, chosen = rest[:GROUPS], rest[GROUPS], rest[GROUPS + 1]
    k = pl.program_id(0)
    b = lax.rem(me_ref[0] + GROUPS - k, GROUPS)
    for j in range(GROUPS):

        @pl.when(k == j)
        def _():
            chosen[...] = solved[j][...]

    used = used_row(count_ref[b])
    seen = gather_points(chosen[...], pid_ref[...])
    remain = [
        (res_ref[a : a + 1, :] - jnp.sum(jp_ref[a] * seen, axis=0, keepdims=True)) * used
        for a in range(2)
    ]
    cam = jc_ref[0] * remain[0] + jc_ref[1] * remain[1]
    cam = jnp.concatenate([cam, jnp.zeros((2, CAP), F32)], axis=0)
    table = one_hot(fid_ref[...].astype(F32), FR)
    sums = lax.dot_general(
        halves(cam), table, (((1,), (1,)), ((), ())), preferred_element_type=F32
    )
    sums = sums[0:CP] + sums[8 : 8 + CP]

    @pl.when(k == 0)
    def _():
        out_ref[...] = sums

    @pl.when(k > 0)
    def _():
        out_ref[...] += sums


def apply_precond(pre_ref, vec):
    return jnp.sum(pre_ref[...] * vec[None], axis=1)


def start_kernel(a_ref, b_ref, c_ref, d_ref, pre_ref, r_ref, z_ref):
    rhs = a_ref[...] + b_ref[...] + c_ref[...] + d_ref[...]
    r_ref[...] = rhs
    z_ref[...] = apply_precond(pre_ref, rhs)


def operator(last_ref, own_ref, left_ref, right_ref, band_ref, edge_ref, edge_left_ref):
    own = own_ref[...]
    padded = jnp.concatenate([left_ref[...], own, right_ref[...]], axis=1)
    totals = [jnp.zeros((CP, FR), F32) for _ in range(CP)]
    for k in range(BANDW):
        at = FR - REACH + k
        shifted = padded[:, at : at + FR]
        for i in range(CP):
            totals[i] = totals[i] + band_ref[k, i] * shifted
    banded = jnp.concatenate([jnp.sum(t, axis=0, keepdims=True) for t in totals], axis=0)
    lane = lax.broadcasted_iota(jnp.int32, (1, FR), 1)
    here = jnp.where((lane == FR - 1) & (last_ref[0] == 1), 0.0, edge_ref[...])
    prev = jnp.concatenate([edge_left_ref[...], here], axis=1)[:, FR - 1 : 2 * FR - 1]
    before = padded[:, FR - 1 : 2 * FR - 1]
    after = padded[:, FR + 1 : 2 * FR + 1]
    return banded + prev * (own - before) + here * (own - after)


def first_kernel(last_ref, z_ref, zl_ref, zr_ref, band_ref, e_ref, el_ref, pre_ref, w_ref, u_ref):
    image = operator(last_ref, z_ref, zl_ref, zr_ref, band_ref, e_ref, el_ref)
    w_ref[...] = image
    u_ref[...] = apply_precond(pre_ref, image)


def second_kernel(
    last_ref, u_ref, ul_ref, ur_ref, band_ref, e_ref, el_ref, r_ref, z_ref, w_ref, out_ref
):
    y = operator(last_ref, u_ref, ul_ref, ur_ref, band_ref, e_ref, el_ref)
    r, z, w, u = r_ref[...], z_ref[...], w_ref[...], u_ref[...]
    lane = lax.broadcasted_iota(jnp.int32, (1, 128), 1)
    row = jnp.zeros((1, 128), F32)
    for at, (one, two) in enumerate(((r, z), (z, w), (r, u), (w, u), (z, y), (u, y))):
        total = jnp.sum(jnp.sum(one * two, axis=0, keepdims=True), axis=1, keepdims=True)
        row = row + jnp.where(lane == at, total, 0.0)
    out_ref[...] = jnp.broadcast_to(row, out_ref.shape)


def back_kernel(me_ref, count_ref, pid_ref, fid_ref, jp_ref, jc_ref, z_ref, u_ref, *outs):
    k = pl.program_id(0)
    b = lax.rem(me_ref[0] + GROUPS - 1 - k, GROUPS)
    used = used_row(count_ref[b])
    zero = jnp.zeros((2, FR), F32)
    stacked = jnp.concatenate([z_ref[...], zero, u_ref[...], zero], axis=0)
    table = one_hot(fid_ref[...].astype(F32), FR)
    got = lax.dot_general(
        halves(stacked), table, (((1,), (0,)), ((), ())), preferred_element_type=F32
    )
    got = got[:16] + got[16:]
    terms = []
    for v in range(2):
        seen = got[v * 8 : v * 8 + CP]
        pair = [jnp.sum(jc_ref[a] * seen, axis=0, keepdims=True) * used for a in range(2)]
        terms.append(jp_ref[0] * pair[0] + jp_ref[1] * pair[1])
    sums = scatter_points(jnp.concatenate(terms, axis=0), pid_ref[...])
    for j in range(GROUPS):

        @pl.when(k == j)
        def _():
            outs[j][...] = sums


def final_kernel(g_ref, z_ref, u_ref, ps_ref, a_ref, b_ref, c_ref, d_ref, inv_ref, cam_ref, pt_ref):
    row = jnp.sum(g_ref[...], axis=0, keepdims=True)
    rz, zw, ru, wu, zy, uy = [row[:, i : i + 1] for i in range(6)]
    a0 = rz / zw
    inner = rz - a0 * (ru + zw) + a0 * a0 * wu
    beta = 1.0 + inner / rz
    curve = beta * beta * zw - beta * a0 * (zy + wu) + a0 * a0 * uy
    a1 = inner / curve
    c0 = a0 + a1 * beta
    c1 = -a1 * a0
    cam_ref[...] = c0 * z_ref[...] + c1 * u_ref[...]
    both = a_ref[...] + b_ref[...] + c_ref[...] + d_ref[...]
    grad = c0 * both[:Q] + c1 * both[Q:]
    pt_ref[...] = ps_ref[...] - jnp.sum(inv_ref[...] * grad[None], axis=1)


def shifted(value, axis, step):
    count = lax.axis_size(axis)
    return lax.ppermute(value, axis, [(i, (i + step) % count) for i in range(count)])


def beside(value):
    count = lax.axis_size("frames")
    up = [(i, i + 1) for i in range(count - 1)]
    down = [(i + 1, i) for i in range(count - 1)]
    return lax.ppermute(value, "frames", up), lax.ppermute(value, "frames", down)


def sds(*shape):
    return jax.ShapeDtypeStruct(shape, F32)


def cost(flops, moved):
    return pl.CostEstimate(flops=flops, bytes_accessed=moved, transcendentals=0)


def blocked(kernel, args, specs, outs, out_specs, name, scratch=(), est=None):
    def call(me, count):
        return pl.pallas_call(
            kernel,
            grid_spec=pltpu.PrefetchScalarGridSpec(
                num_scalar_prefetch=2,
                grid=(GROUPS,),
                in_specs=specs,
                out_specs=out_specs,
                scratch_shapes=list(scratch),
            ),
            out_shape=outs,
            cost_estimate=est,
            name=name,
        )(me, count, *args)

    return call


def lanes_spec(shape, turn):
    lead = shape[:-1]

    def index(k, me, count):
        return (0,) * len(lead) + (lax.rem(me[0] + GROUPS + turn(k), GROUPS),)

    return pl.BlockSpec(lead + (CAP,), index)


def whole_spec(shape):
    return pl.BlockSpec(shape, lambda k, me, count: (0,) * len(shape))


def plain(kernel, outs, smem, args, name, est=None):
    specs = [
        pl.BlockSpec(memory_space=pltpu.SMEM if i in smem else pltpu.VMEM) for i in range(len(args))
    ]
    out_specs = jax.tree.map(lambda _: pl.BlockSpec(memory_space=pltpu.VMEM), outs)
    return pl.pallas_call(
        kernel, in_specs=specs, out_specs=out_specs, out_shape=outs, cost_estimate=est, name=name
    )(*args)


def local(
    obs_count,
    obs_point,
    obs_frame,
    jac_cam,
    jac_point,
    residual,
    point_inv,
    band,
    edge_weight,
    precond,
):
    slots = obs_point.shape[0]
    pid = obs_point.reshape(1, slots)
    fid = obs_frame.reshape(1, slots)
    me = lax.axis_index("points").astype(jnp.int32).reshape(1)
    count = lax.axis_size("frames")
    last = (lax.axis_index("frames") == count - 1).astype(jnp.int32).reshape(1)
    edge = edge_weight.reshape(1, FR)
    edge_left = lax.ppermute(edge, "frames", [(i, i + 1) for i in range(count - 1)])

    ahead = lambda k: GROUPS - 1 - k
    behind = lambda k: -k

    sums = blocked(
        grad_kernel,
        (pid, residual, jac_point),
        [lanes_spec((1, slots), ahead), lanes_spec((2, slots), ahead), lanes_spec((2, Q, slots), ahead)],
        [sds(Q, PT)] * GROUPS,
        [whole_spec((Q, PT))] * GROUPS,
        "point_grad",
        est=cost(2 * 192 * 256 * 8192, 2 * 24 * 8192 * 4),
    )(me, obs_count)
    got = [shifted(sums[GROUPS - 1 - s], "points", s) for s in (3, 2, 1)] + [sums[GROUPS - 1]]

    inv_spec = [pl.BlockSpec((Q, 256), lambda k: (0, k))] * GROUPS + [
        pl.BlockSpec((Q, Q, 256), lambda k: (0, 0, k))
    ]
    solved = pl.pallas_call(
        solve_kernel,
        grid=(PT // 256,),
        in_specs=inv_spec,
        out_specs=pl.BlockSpec((Q, 256), lambda k: (0, k)),
        out_shape=sds(Q, PT),
        cost_estimate=cost(2 * Q * Q * PT, Q * Q * PT * 4),
        name="point_solve",
    )(*got, point_inv)
    all_solved = [solved] + [shifted(solved, "points", s) for s in (1, 2, 3)]

    partial = blocked(
        rhs_kernel,
        (pid, fid, residual, jac_point, jac_cam, *all_solved),
        [
            lanes_spec((1, slots), behind),
            lanes_spec((1, slots), behind),
            lanes_spec((2, slots), behind),
            lanes_spec((2, Q, slots), behind),
            lanes_spec((2, CP, slots), behind),
        ]
        + [whole_spec((Q, PT))] * GROUPS,
        sds(CP, FR),
        whole_spec((CP, FR)),
        "camera_rhs",
        scratch=[pltpu.VMEM((Q, PT), F32)],
        est=cost(2 * 256 * 256 * 8192, 2 * 32 * 8192 * 4),
    )(me, obs_count)
    parts = [partial] + [shifted(partial, "points", s) for s in (1, 2, 3)]

    rhs, z = plain(
        start_kernel, [sds(CP, FR)] * 2, (), (*parts, precond), "start", est=cost(20000, 100000)
    )
    z_left, z_right = beside(z)
    w, u = plain(
        first_kernel,
        [sds(CP, FR)] * 2,
        (0,),
        (last, z, z_left, z_right, band, edge, edge_left, precond),
        "operator_one",
        est=cost(2 * 127 * 36 * 256, 127 * 48 * 256 * 4),
    )
    u_left, u_right = beside(u)
    back = blocked(
        back_kernel,
        (pid, fid, jac_point, jac_cam, z, u),
        [
            lanes_spec((1, slots), ahead),
            lanes_spec((1, slots), ahead),
            lanes_spec((2, Q, slots), ahead),
            lanes_spec((2, CP, slots), ahead),
            whole_spec((CP, FR)),
            whole_spec((CP, FR)),
        ],
        [sds(2 * Q, PT)] * GROUPS,
        [whole_spec((2 * Q, PT))] * GROUPS,
        "back_terms",
        est=cost(2 * 400 * 256 * 8192, 2 * 32 * 8192 * 4),
    )(me, obs_count)
    returned = [shifted(back[GROUPS - 1 - s], "points", s) for s in (3, 2, 1)] + [back[GROUPS - 1]]
    gram = plain(
        second_kernel,
        sds(count, 128),
        (0,),
        (last, u, u_left, u_right, band, edge, edge_left, rhs, z, w),
        "operator_two",
        est=cost(2 * 127 * 36 * 256, 127 * 48 * 256 * 4),
    )
    gram = lax.all_to_all(gram, "frames", split_axis=0, concat_axis=0, tiled=True)

    whole = lambda shape: pl.BlockSpec(shape, lambda k: (0,) * len(shape))
    camera_step, point_step = pl.pallas_call(
        final_kernel,
        grid=(PT // 256,),
        in_specs=[
            whole((count, 128)),
            whole((CP, FR)),
            whole((CP, FR)),
            pl.BlockSpec((Q, 256), lambda k: (0, k)),
        ]
        + [pl.BlockSpec((2 * Q, 256), lambda k: (0, k))] * GROUPS
        + [pl.BlockSpec((Q, Q, 256), lambda k: (0, 0, k))],
        out_specs=[whole((CP, FR)), pl.BlockSpec((Q, 256), lambda k: (0, k))],
        out_shape=[sds(CP, FR), sds(Q, PT)],
        cost_estimate=cost(2 * Q * Q * PT, Q * Q * PT * 4),
        name="final",
    )(gram, z, u, solved, *returned, point_inv)
    return camera_step, point_step


def solution(mesh):
    placed = (
        P(("frames", "points")),
        P(("frames", "points")),
        P(("frames", "points")),
        P(None, None, ("frames", "points")),
        P(None, None, ("frames", "points")),
        P(None, ("frames", "points")),
        P(None, None, ("frames", "points")),
        P(None, None, None, "frames"),
        P("frames"),
        P(None, None, "frames"),
    )
    return jax.shard_map(
        local,
        mesh=mesh,
        in_specs=placed,
        out_specs=(P(None, "frames"), P(None, ("frames", "points"))),
        check_vma=False,
    )
```

```python
import functools

import jax
import jax.numpy as jnp
from jax import lax
from jax.experimental import pallas as pl
from jax.experimental.pallas import tpu as pltpu
from jax.sharding import PartitionSpec as P

F32 = jnp.float32
BF16 = jnp.bfloat16
CP = 6
Q = 24
BANDW = 127
REACH = 63
FR = 256
PT = 1024
CAP = 2048
GROUPS = 4
LO = 256
HI = PT // LO
LIMIT = pltpu.CompilerParams(vmem_limit_bytes=12 * 2**20)


def halves(x):
    lead = x.astype(BF16).astype(F32)
    return jnp.concatenate([lead, x - lead], axis=0).astype(BF16)


def one_hot(row, rows):
    n = row.shape[1]
    index = lax.broadcasted_iota(jnp.int32, (rows, 128), 0).astype(F32).astype(BF16)
    row = row.astype(BF16)
    cols = []
    for c in range(n // 128):
        here = jnp.broadcast_to(row[:, c * 128 : (c + 1) * 128], (rows, 128))
        cols.append(jnp.where(index == here, jnp.ones_like(index), jnp.zeros_like(index)))
    return jnp.concatenate(cols, axis=1)


def split_ids(ids):
    hi = lax.shift_right_logical(ids, 8)
    lo = lax.bitwise_and(ids, LO - 1)
    return hi.astype(F32), lo.astype(F32)


def used_row(count):
    lane = lax.broadcasted_iota(jnp.int32, (1, CAP), 1)
    return (lane < count).astype(F32)


def scatter_points(terms, ids):
    n = terms.shape[0]
    hi, lo = split_ids(ids)
    parts = halves(terms)
    table = one_hot(lo, LO)
    rows = []
    for h in range(HI):
        mask = jnp.broadcast_to((hi == h).astype(F32), (2 * n, CAP)).astype(BF16)
        rows.append(parts * mask)
    sums = lax.dot_general(
        jnp.concatenate(rows, axis=0), table, (((1,), (1,)), ((), ())), preferred_element_type=F32
    )
    out = []
    for h in range(HI):
        block = sums[h * 2 * n : (h + 1) * 2 * n]
        out.append(block[:n] + block[n:])
    return jnp.concatenate(out, axis=1)


def gather_points(values, ids):
    n = values.shape[0]
    hi, lo = split_ids(ids)
    parts = halves(values)
    table = one_hot(lo, LO)
    stacked = jnp.concatenate([parts[:, h * LO : (h + 1) * LO] for h in range(HI)], axis=0)
    got = lax.dot_general(stacked, table, (((1,), (0,)), ((), ())), preferred_element_type=F32)
    total = None
    for h in range(HI):
        block = got[h * 2 * n : (h + 1) * 2 * n]
        term = (block[:n] + block[n:]) * (hi == h).astype(F32)
        total = term if total is None else total + term
    return total


def block_at(turn):
    return lax.rem(lax.axis_index("points") + GROUPS + turn, GROUPS)


def lanes(b):
    return pl.ds(pl.multiple_of(b * CAP, CAP), CAP)


def grad_kernel(count_ref, ids_hbm, res_hbm, jp_hbm, *rest):
    outs, (ids_ref, res_ref, jp_ref, sems) = rest[:GROUPS], rest[GROUPS:]
    small = [
        pltpu.make_async_copy(ids_hbm, ids_ref, sems.at[GROUPS]),
        pltpu.make_async_copy(res_hbm, res_ref, sems.at[GROUPS + 1]),
    ]
    blocks = [block_at(GROUPS - 1 - j) for j in range(GROUPS)]
    large = [
        pltpu.make_async_copy(jp_hbm.at[:, :, lanes(b)], jp_ref.at[j], sems.at[j])
        for j, b in enumerate(blocks)
    ]
    for copy in small + large:
        copy.start()
    for copy in small:
        copy.wait()
    for j, b in enumerate(blocks):
        at = lanes(b)
        large[j].wait()
        res = res_ref[:, at] * used_row(count_ref[b])
        terms = jp_ref[j, 0] * res[0:1] + jp_ref[j, 1] * res[1:2]
        outs[j][...] = scatter_points(terms, ids_ref[:, at])


def solve_kernel(a_ref, b_ref, c_ref, d_ref, inv_ref, out_ref):
    grad = a_ref[...] + b_ref[...] + c_ref[...] + d_ref[...]
    out_ref[...] = jnp.sum(inv_ref[...] * grad[None], axis=1)


def rhs_kernel(turn, count_ref, pid_ref, fid_ref, res_ref, jp_ref, jc_ref, *rest):
    solved_ref, out_ref = rest[-2:]
    b = block_at(turn)
    at = lanes(b)
    used = used_row(count_ref[b])
    seen = gather_points(solved_ref[...], pid_ref[:, at])
    remain = [
        (res_ref[a : a + 1, at] - jnp.sum(jp_ref[a, :, at] * seen, axis=0, keepdims=True)) * used
        for a in range(2)
    ]
    cam = jc_ref[0, :, at] * remain[0] + jc_ref[1, :, at] * remain[1]
    cam = jnp.concatenate([cam, jnp.zeros((2, CAP), F32)], axis=0)
    table = one_hot(fid_ref[:, at].astype(F32), FR)
    sums = lax.dot_general(
        halves(cam), table, (((1,), (1,)), ((), ())), preferred_element_type=F32
    )
    total = sums[0:CP] + sums[8 : 8 + CP]
    out_ref[...] = total if len(rest) == 2 else total + rest[0][...]


def apply_precond(pre_ref, vec):
    return jnp.sum(pre_ref[...] * vec[None], axis=1)


def start_kernel(a_ref, b_ref, c_ref, d_ref, pre_ref, edge_ref, r_ref, z_ref):
    rhs = a_ref[...] + b_ref[...] + c_ref[...] + d_ref[...]
    r_ref[...] = rhs
    lane = lax.broadcasted_iota(jnp.int32, (1, FR), 1)
    last = lax.axis_index("frames") == lax.axis_size("frames") - 1
    edge = edge_ref[...] * jnp.where((lane == FR - 1) & last, 0.0, 1.0)
    z = apply_precond(pre_ref, rhs)
    z_ref[...] = jnp.concatenate([z, edge, jnp.zeros((1, FR), F32)], axis=0)


def steps_of(row, width):
    n = row.shape[1]
    sub = lax.broadcasted_iota(jnp.int32, (8, n), 0)
    x = jnp.broadcast_to(row, (8, n))
    for bit in (1, 2, 4):
        x = jnp.where((sub & bit) != 0, pltpu.roll(x, n - bit, 1), x)
    return x


def banded_sums(band_ref, rows, tiles, first=None):
    totals = [None] * CP
    ends = [None] * CP
    for j in range(CP):
        stepped = steps_of(rows[j], 0)
        for t in tiles:
            at = 128 - REACH + 8 * t
            shifted = stepped[:, at : at + FR]
            if t == first:
                sub = lax.broadcasted_iota(jnp.int32, (8, FR), 0)
                shifted = jnp.where(sub == 7, 0.5 * shifted, 0.0)
            for i in range(CP):
                if 8 * t + 8 <= BANDW:
                    term = band_ref[i, j, 8 * t : 8 * t + 8, :] * shifted
                    totals[i] = term if totals[i] is None else totals[i] + term
                else:
                    count = BANDW - 8 * t
                    term = band_ref[i, j, 8 * t : BANDW, :] * shifted[:count]
                    ends[i] = term if ends[i] is None else ends[i] + term
    return jnp.concatenate(
        [
            jnp.sum(t, axis=0, keepdims=True) + jnp.sum(e, axis=0, keepdims=True)
            for t, e in zip(totals, ends)
        ],
        axis=0,
    )


def first_kernel(z_ref, left_ref, right_ref, band_ref, pre_ref, w_ref, u_ref):
    padded = jnp.concatenate([left_ref[...], z_ref[...], right_ref[...]], axis=1)
    near = padded[:, FR - 128 : 2 * FR + 128]
    banded = banded_sums(band_ref, [near[j : j + 1] for j in range(CP)], range(16))
    own = z_ref[:CP, :]
    here = z_ref[CP : CP + 1, :]
    prev = padded[CP : CP + 1, FR - 1 : 2 * FR - 1]
    before = padded[:CP, FR - 1 : 2 * FR - 1]
    after = padded[:CP, FR + 1 : 2 * FR + 1]
    image = banded + prev * (own - before) + here * (own - after)
    w_ref[...] = image
    u = apply_precond(pre_ref, image)
    u_ref[...] = jnp.concatenate([u, jnp.zeros((2, FR), F32)], axis=0)


def second_kernel(u_ref, right_ref, band_ref, r_ref, z_ref, w_ref, out_ref):
    ahead = jnp.concatenate([u_ref[...], right_ref[...]], axis=1)
    near = jnp.concatenate([jnp.zeros((8, 128), F32), ahead[:, : FR + 128]], axis=1)
    upper = banded_sums(band_ref, [near[j : j + 1] for j in range(CP)], range(7, 16), first=7)
    u, z, w, r = u_ref[:CP, :], z_ref[:CP, :], w_ref[...], r_ref[...]
    edge = z_ref[CP : CP + 1, :]
    step = u - ahead[:CP, 1 : FR + 1]
    lane = lax.broadcasted_iota(jnp.int32, (1, 128), 1)
    row = jnp.zeros((1, 128), F32)
    for at, term in enumerate((r * z, z * w, w * u, 2.0 * u * upper + edge * step * step)):
        total = jnp.sum(jnp.sum(term, axis=0, keepdims=True), axis=1, keepdims=True)
        row = row + jnp.where(lane == at, total, 0.0)
    out_ref[...] = jnp.broadcast_to(row, out_ref.shape)


def back_kernel(count_ref, pid_ref, fid_ref, jp_ref, jc_ref, z_ref, u_ref, *outs):
    parts = halves(jnp.concatenate([z_ref[...], u_ref[...]], axis=0))
    for j in range(GROUPS):
        b = block_at(GROUPS - 1 - j)
        at = lanes(b)
        used = used_row(count_ref[b])
        table = one_hot(fid_ref[:, at].astype(F32), FR)
        got = lax.dot_general(parts, table, (((1,), (0,)), ((), ())), preferred_element_type=F32)
        got = got[:16] + got[16:]
        terms = []
        for v in range(2):
            seen = got[v * 8 : v * 8 + CP]
            pair = [
                jnp.sum(jc_ref[a, :, at] * seen, axis=0, keepdims=True) * used for a in range(2)
            ]
            terms.append(jp_ref[0, :, at] * pair[0] + jp_ref[1, :, at] * pair[1])
        outs[j][...] = scatter_points(jnp.concatenate(terms, axis=0), pid_ref[:, at])


def undo_kernel(a_ref, b_ref, c_ref, d_ref, inv_ref, z_ref, u_ref):
    both = a_ref[...] + b_ref[...] + c_ref[...] + d_ref[...]
    z_ref[...] = jnp.sum(inv_ref[...] * both[None, :Q], axis=1)
    u_ref[...] = jnp.sum(inv_ref[...] * both[None, Q:], axis=1)


def final_kernel(g_ref, z_ref, u_ref, ps_ref, pz_ref, pu_ref, cam_ref, pt_ref):
    row = jnp.sum(g_ref[...], axis=0, keepdims=True)
    rz, zw, wu, uy = [row[:, i : i + 1] for i in range(4)]
    a0 = rz / zw
    inner = a0 * a0 * wu - rz
    beta = 1.0 + inner / rz
    curve = beta * beta * zw - 2.0 * beta * a0 * wu + a0 * a0 * uy
    a1 = inner / curve
    c0 = a0 + a1 * beta
    c1 = -a1 * a0
    cam_ref[...] = c0 * z_ref[:CP, :] + c1 * u_ref[:CP, :]
    pt_ref[...] = ps_ref[...] - c0 * pz_ref[...] - c1 * pu_ref[...]


def shifted(value, axis, step):
    count = lax.axis_size(axis)
    return lax.ppermute(value, axis, [(i, (i + step) % count) for i in range(count)])


def beside(value):
    count = lax.axis_size("frames")
    up = [(i, i + 1) for i in range(count - 1)]
    down = [(i + 1, i) for i in range(count - 1)]
    return lax.ppermute(value, "frames", up), lax.ppermute(value, "frames", down)


def sds(*shape):
    return jax.ShapeDtypeStruct(shape, F32)


def cost(flops, moved):
    return pl.CostEstimate(flops=flops, bytes_accessed=moved, transcendentals=0)


def plain(kernel, outs, args, name, smem=(), raw=(), scratch=(), est=None, params=LIMIT):
    space = lambda i: pltpu.SMEM if i in smem else pltpu.HBM if i in raw else pltpu.VMEM
    specs = [pl.BlockSpec(memory_space=space(i)) for i in range(len(args))]
    out_specs = jax.tree.map(lambda _: pl.BlockSpec(memory_space=pltpu.VMEM), outs)
    return pl.pallas_call(
        kernel,
        in_specs=specs,
        out_specs=out_specs,
        out_shape=outs,
        scratch_shapes=list(scratch),
        cost_estimate=est,
        compiler_params=params,
        name=name,
    )(*args)


def local(
    obs_count,
    obs_point,
    obs_frame,
    jac_cam,
    jac_point,
    residual,
    point_inv,
    band,
    edge_weight,
    precond,
):
    slots = obs_point.shape[0]
    pid = obs_point.reshape(1, slots)
    fid = obs_frame.reshape(1, slots)
    count = lax.axis_size("frames")
    edge = edge_weight.reshape(1, FR)
    bands = jnp.transpose(band, (1, 2, 0, 3))

    sums = plain(
        grad_kernel,
        [sds(Q, PT)] * GROUPS,
        (obs_count, pid, residual, jac_point),
        "point_grad",
        smem=(0,),
        raw=(1, 2, 3),
        scratch=[
            pltpu.VMEM((1, slots), jnp.int32),
            pltpu.VMEM((2, slots), F32),
            pltpu.VMEM((GROUPS, 2, Q, CAP), F32),
            pltpu.SemaphoreType.DMA((GROUPS + 2,)),
        ],
        est=cost(2 * 192 * 256 * 8192, 2 * 24 * 8192 * 4),
        params=None,
    )
    got = [shifted(sums[GROUPS - 1 - s], "points", s) for s in (3, 2, 1)] + [sums[GROUPS - 1]]
    solved = plain(
        solve_kernel, sds(Q, PT), (*got, point_inv), "point_solve", est=cost(2 * Q * Q * PT, Q * Q * PT * 4)
    )
    partial = ()
    for s in (0, 1, 3, 2):
        piece = shifted(solved, "points", s) if s else solved
        partial = (
            plain(
                functools.partial(rhs_kernel, -s),
                sds(CP, FR),
                (obs_count, pid, fid, residual, jac_point, jac_cam, *partial, piece),
                "camera_rhs",
                smem=(0,),
                est=cost(2 * 256 * 256 * 2048, 2 * 32 * 2048 * 4),
            ),
        )
    (partial,) = partial
    parts = [partial] + [shifted(partial, "points", s) for s in (1, 2, 3)]

    rhs, z = plain(
        start_kernel,
        [sds(CP, FR), sds(8, FR)],
        (*parts, precond, edge),
        "start",
        est=cost(20000, 100000),
    )
    z_left, z_right = beside(z)
    w, u = plain(
        first_kernel,
        [sds(CP, FR), sds(8, FR)],
        (z, z_left, z_right, bands, precond),
        "operator_one",
        est=cost(2 * 127 * 36 * 256, 127 * 36 * 256 * 4),
    )
    u_right = lax.ppermute(u, "frames", [(i + 1, i) for i in range(count - 1)])
    back = plain(
        back_kernel,
        [sds(2 * Q, PT)] * GROUPS,
        (obs_count, pid, fid, jac_point, jac_cam, z, u),
        "back_terms",
        smem=(0,),
        est=cost(2 * 400 * 256 * 8192, 2 * 32 * 8192 * 4),
    )
    returned = [shifted(back[GROUPS - 1 - s], "points", s) for s in (3, 2, 1)] + [back[GROUPS - 1]]
    gram = plain(
        second_kernel,
        sds(count, 128),
        (u, u_right, bands, rhs, z, w),
        "operator_two",
        est=cost(127 * 36 * 256, 127 * 18 * 256 * 4),
    )
    gram = lax.all_to_all(gram, "frames", split_axis=0, concat_axis=0, tiled=True)
    undo_z, undo_u = plain(
        undo_kernel,
        [sds(Q, PT)] * 2,
        (*returned, point_inv),
        "undo",
        est=cost(4 * Q * Q * PT, Q * Q * PT * 4),
    )
    camera_step, point_step = plain(
        final_kernel,
        [sds(CP, FR), sds(Q, PT)],
        (gram, z, u, solved, undo_z, undo_u),
        "final",
        est=cost(6 * Q * PT, 6 * Q * PT * 4),
    )
    return camera_step, point_step


def solution(mesh):
    placed = (
        P(("frames", "points")),
        P(("frames", "points")),
        P(("frames", "points")),
        P(None, None, ("frames", "points")),
        P(None, None, ("frames", "points")),
        P(None, ("frames", "points")),
        P(None, None, ("frames", "points")),
        P(None, None, None, "frames"),
        P("frames"),
        P(None, None, "frames"),
    )
    return jax.shard_map(
        local,
        mesh=mesh,
        in_specs=placed,
        out_specs=(P(None, "frames"), P(None, ("frames", "points"))),
        check_vma=False,
    )
```

```python
import functools

import jax
import jax.numpy as jnp
from jax import lax
from jax.experimental import pallas as pl
from jax.experimental.pallas import tpu as pltpu
from jax.sharding import PartitionSpec as P


F32 = jnp.float32
BF16 = jnp.bfloat16
CP = 6
Q = 24
BANDW = 127
REACH = 63
FR = 256
PT = 1024
CAP = 2048
GROUPS = 4
LO = 256
HI = PT // LO
LIMIT = pltpu.CompilerParams(vmem_limit_bytes=12 * 2**20)


def halves(x):
    lead = x.astype(BF16).astype(F32)
    return jnp.concatenate([lead, x - lead], axis=0).astype(BF16)


def one_hot(row, rows):
    n = row.shape[1]
    index = lax.broadcasted_iota(jnp.int32, (rows, 128), 0).astype(F32).astype(BF16)
    row = row.astype(BF16)
    cols = []
    for c in range(n // 128):
        here = jnp.broadcast_to(row[:, c * 128 : (c + 1) * 128], (rows, 128))
        cols.append(jnp.where(index == here, jnp.ones_like(index), jnp.zeros_like(index)))
    return jnp.concatenate(cols, axis=1)


def split_ids(ids):
    hi = lax.shift_right_logical(ids, 8)
    lo = lax.bitwise_and(ids, LO - 1)
    return hi.astype(F32), lo.astype(F32)


def used_or(ids, count, other):
    lane = lax.broadcasted_iota(jnp.int32, ids.shape, 1)
    return jnp.where(lane < count, ids, other)


def scatter_points(terms, ids):
    n = terms.shape[0]
    hi, lo = split_ids(ids)
    parts = halves(terms)
    table = one_hot(lo, LO)
    rows = []
    for h in range(HI):
        mask = jnp.broadcast_to((hi == h).astype(F32), (2 * n, CAP)).astype(BF16)
        rows.append(parts * mask)
    sums = lax.dot_general(
        jnp.concatenate(rows, axis=0), table, (((1,), (1,)), ((), ())), preferred_element_type=F32
    )
    out = []
    for h in range(HI):
        block = sums[h * 2 * n : (h + 1) * 2 * n]
        out.append(block[:n] + block[n:])
    return jnp.concatenate(out, axis=1)


def gather_points(values, ids):
    n = values.shape[0]
    hi, lo = split_ids(ids)
    parts = halves(values)
    table = one_hot(lo, LO)
    stacked = jnp.concatenate([parts[:, h * LO : (h + 1) * LO] for h in range(HI)], axis=0)
    got = lax.dot_general(stacked, table, (((1,), (0,)), ((), ())), preferred_element_type=F32)
    total = None
    for h in range(HI):
        block = got[h * 2 * n : (h + 1) * 2 * n]
        term = (block[:n] + block[n:]) * (hi == h).astype(F32)
        total = term if total is None else total + term
    return total


def block_at(turn):
    return lax.rem(lax.axis_index("points") + GROUPS + turn, GROUPS)


def lanes(b):
    return pl.ds(pl.multiple_of(b * CAP, CAP), CAP)


def fetch(pairs, sems):
    copies = [pltpu.make_async_copy(src, dst, sems.at[i]) for i, (src, dst) in enumerate(pairs)]
    for copy in copies:
        copy.start()
    return copies


def grad_kernel(count_hbm, ids_hbm, res_hbm, jp_hbm, *rest):
    far = GROUPS - 1
    outs, (count_ref, ids_ref, res_ref, jp_ref, sems) = rest[:far], rest[far:]
    blocks = [block_at(GROUPS - 1 - j) for j in range(far)]
    large = [(jp_hbm.at[:, :, lanes(b)], jp_ref.at[j]) for j, b in enumerate(blocks)]
    small = [(count_hbm, count_ref), (ids_hbm, ids_ref), (res_hbm, res_ref)]
    copies = fetch(small + large, sems)
    for copy in copies[:3]:
        copy.wait()
    for j, b in enumerate(blocks):
        at = lanes(b)
        copies[3 + j].wait()
        terms = jp_ref[j, 0] * res_ref[0:1, at] + jp_ref[j, 1] * res_ref[1:2, at]
        outs[j][...] = scatter_points(terms, used_or(ids_ref[:, at], count_ref[b], PT))


def own_kernel(
    after_ref, count_hbm, pid_hbm, fid_hbm, res_hbm, jp_hbm, out_ref, pid_out, fid_out,
    count_ref, res_ref, jp_ref, sems,
):
    b = block_at(0)
    at = lanes(b)
    copies = fetch(
        [
            (count_hbm, count_ref),
            (pid_hbm, pid_out),
            (fid_hbm, fid_out),
            (res_hbm.at[:, at], res_ref),
            (jp_hbm.at[:, :, at], jp_ref),
        ],
        sems,
    )
    for copy in copies:
        copy.wait()
    for g in range(GROUPS):
        here = slice(g * CAP, (g + 1) * CAP)
        pid_out[:, here] = used_or(pid_out[:, here], count_ref[g], PT)
        fid_out[:, here] = used_or(fid_out[:, here], count_ref[g], FR)
    terms = jp_ref[0] * res_ref[0:1, :] + jp_ref[1] * res_ref[1:2, :]
    out_ref[...] = scatter_points(terms, pid_out[:, at])


def solve_kernel(a_ref, b_ref, c_ref, d_ref, inv_ref, out_ref):
    grad = a_ref[...] + b_ref[...] + c_ref[...] + d_ref[...]
    out_ref[...] = jnp.sum(inv_ref[...] * grad[None], axis=1)


def rhs_kernel(turn, pid_ref, fid_ref, res_ref, jp_ref, jc_ref, *rest):
    solved_ref, out_ref = rest[-2:]
    b = block_at(turn)
    at = lanes(b)
    seen = gather_points(solved_ref[...], pid_ref[:, at])
    remain = [
        res_ref[a : a + 1, at] - jnp.sum(jp_ref[a, :, at] * seen, axis=0, keepdims=True)
        for a in range(2)
    ]
    cam = jc_ref[0, :, at] * remain[0] + jc_ref[1, :, at] * remain[1]
    cam = jnp.concatenate([cam, jnp.zeros((2, CAP), F32)], axis=0)
    table = one_hot(fid_ref[:, at].astype(F32), FR)
    sums = lax.dot_general(
        halves(cam), table, (((1,), (1,)), ((), ())), preferred_element_type=F32
    )
    total = sums[0:CP] + sums[8 : 8 + CP]
    out_ref[...] = total if len(rest) == 2 else total + rest[0][...]


def apply_precond(pre_ref, vec):
    return jnp.sum(pre_ref[...] * vec[None], axis=1)


def start_kernel(a_ref, b_ref, c_ref, d_ref, pre_ref, edge_ref, r_ref, z_ref):
    rhs = a_ref[...] + b_ref[...] + c_ref[...] + d_ref[...]
    r_ref[...] = rhs
    lane = lax.broadcasted_iota(jnp.int32, (1, FR), 1)
    last = lax.axis_index("frames") == lax.axis_size("frames") - 1
    edge = edge_ref[...] * jnp.where((lane == FR - 1) & last, 0.0, 1.0)
    z = apply_precond(pre_ref, rhs)
    z_ref[...] = jnp.concatenate([z, edge, jnp.zeros((1, FR), F32)], axis=0)


def steps_of(row):
    n = row.shape[1]
    sub = lax.broadcasted_iota(jnp.int32, (8, n), 0)
    x = jnp.broadcast_to(row, (8, n))
    for bit in (1, 2, 4):
        x = jnp.where((sub & bit) != 0, pltpu.roll(x, n - bit, 1), x)
    return x


def banded_sums(band_ref, rows, tiles, first=None):
    totals = [None] * CP
    ends = [None] * CP
    for j in range(CP):
        stepped = steps_of(rows[j])
        for t in tiles:
            at = 128 - REACH + 8 * t
            shifted = stepped[:, at : at + FR]
            if t == first:
                sub = lax.broadcasted_iota(jnp.int32, (8, FR), 0)
                shifted = jnp.where(sub == 7, 0.5 * shifted, 0.0)
            for i in range(CP):
                if 8 * t + 8 <= BANDW:
                    term = band_ref[i, j, 8 * t : 8 * t + 8, :] * shifted
                    totals[i] = term if totals[i] is None else totals[i] + term
                else:
                    count = BANDW - 8 * t
                    term = band_ref[i, j, 8 * t : BANDW, :] * shifted[:count]
                    ends[i] = term if ends[i] is None else ends[i] + term
    return jnp.concatenate(
        [
            jnp.sum(t, axis=0, keepdims=True) + jnp.sum(e, axis=0, keepdims=True)
            for t, e in zip(totals, ends)
        ],
        axis=0,
    )


def first_kernel(z_ref, left_ref, right_ref, band_ref, pre_ref, w_ref, u_ref):
    padded = jnp.concatenate([left_ref[...], z_ref[...], right_ref[...]], axis=1)
    near = padded[:, FR - 128 : 2 * FR + 128]
    banded = banded_sums(band_ref, [near[j : j + 1] for j in range(CP)], range(16))
    own = z_ref[:CP, :]
    here = z_ref[CP : CP + 1, :]
    prev = padded[CP : CP + 1, FR - 1 : 2 * FR - 1]
    before = padded[:CP, FR - 1 : 2 * FR - 1]
    after = padded[:CP, FR + 1 : 2 * FR + 1]
    image = banded + prev * (own - before) + here * (own - after)
    w_ref[...] = image
    u = apply_precond(pre_ref, image)
    u_ref[...] = jnp.concatenate([u, jnp.zeros((2, FR), F32)], axis=0)


def second_kernel(u_ref, right_ref, band_ref, r_ref, z_ref, w_ref, out_ref):
    ahead = jnp.concatenate([u_ref[...], right_ref[...]], axis=1)
    near = jnp.concatenate([jnp.zeros((8, 128), F32), ahead[:, : FR + 128]], axis=1)
    upper = banded_sums(band_ref, [near[j : j + 1] for j in range(CP)], range(7, 16), first=7)
    u, z, w, r = u_ref[:CP, :], z_ref[:CP, :], w_ref[...], r_ref[...]
    edge = z_ref[CP : CP + 1, :]
    step = u - ahead[:CP, 1 : FR + 1]
    lane = lax.broadcasted_iota(jnp.int32, (1, 128), 1)
    row = jnp.zeros((1, 128), F32)
    for at, term in enumerate((r * z, z * w, w * u, 2.0 * u * upper + edge * step * step)):
        total = jnp.sum(jnp.sum(term, axis=0, keepdims=True), axis=1, keepdims=True)
        row = row + jnp.where(lane == at, total, 0.0)
    out_ref[...] = jnp.broadcast_to(row, out_ref.shape)


def back_kernel(pid_ref, fid_ref, jp_ref, jc_ref, z_ref, u_ref, *outs):
    parts = halves(jnp.concatenate([z_ref[...], u_ref[...]], axis=0))
    for j in range(GROUPS):
        b = block_at(GROUPS - 1 - j)
        at = lanes(b)
        table = one_hot(fid_ref[:, at].astype(F32), FR)
        got = lax.dot_general(parts, table, (((1,), (0,)), ((), ())), preferred_element_type=F32)
        got = got[:16] + got[16:]
        terms = []
        for v in range(2):
            seen = got[v * 8 : v * 8 + CP]
            pair = [jnp.sum(jc_ref[a, :, at] * seen, axis=0, keepdims=True) for a in range(2)]
            terms.append(jp_ref[0, :, at] * pair[0] + jp_ref[1, :, at] * pair[1])
        outs[j][...] = scatter_points(jnp.concatenate(terms, axis=0), pid_ref[:, at])


def undo_kernel(a_ref, b_ref, c_ref, d_ref, inv_hbm, z_ref, u_ref, inv_ref, sem):
    pltpu.async_copy(inv_hbm, inv_ref, sem).wait()
    both = a_ref[...] + b_ref[...] + c_ref[...] + d_ref[...]
    z_ref[...] = jnp.sum(inv_ref[...] * both[None, :Q], axis=1)
    u_ref[...] = jnp.sum(inv_ref[...] * both[None, Q:], axis=1)


def final_kernel(g_ref, z_ref, u_ref, ps_ref, pz_ref, pu_ref, cam_ref, pt_ref):
    row = jnp.sum(g_ref[...], axis=0, keepdims=True)
    rz, zw, wu, uy = [row[:, i : i + 1] for i in range(4)]
    a0 = rz / zw
    inner = a0 * a0 * wu - rz
    beta = 1.0 + inner / rz
    curve = beta * beta * zw - 2.0 * beta * a0 * wu + a0 * a0 * uy
    a1 = inner / curve
    c0 = a0 + a1 * beta
    c1 = -a1 * a0
    cam_ref[...] = c0 * z_ref[:CP, :] + c1 * u_ref[:CP, :]
    pt_ref[...] = ps_ref[...] - c0 * pz_ref[...] - c1 * pu_ref[...]


def shifted(value, axis, step):
    count = lax.axis_size(axis)
    return lax.ppermute(value, axis, [(i, (i + step) % count) for i in range(count)])


def beside(value):
    count = lax.axis_size("frames")
    up = [(i, i + 1) for i in range(count - 1)]
    down = [(i + 1, i) for i in range(count - 1)]
    return lax.ppermute(value, "frames", up), lax.ppermute(value, "frames", down)


def sds(*shape):
    return jax.ShapeDtypeStruct(shape, F32)


def cost(flops, moved):
    return pl.CostEstimate(flops=flops, bytes_accessed=moved, transcendentals=0)


def plain(kernel, outs, args, smem=(), raw=(), scratch=(), est=None, ):
    space = lambda i: pltpu.SMEM if i in smem else pltpu.HBM if i in raw else pltpu.VMEM
    specs = [pl.BlockSpec(memory_space=space(i)) for i in range(len(args))]
    args = [pltpu.with_memory_space_constraint(x, pltpu.HBM) if i in raw else x for i, x in enumerate(args)]
    out_specs = jax.tree.map(lambda _: pl.BlockSpec(memory_space=pltpu.VMEM), outs)
    return pl.pallas_call(
        kernel,
        in_specs=specs,
        out_specs=out_specs,
        out_shape=outs,
        scratch_shapes=list(scratch),
        cost_estimate=est,
        compiler_params=LIMIT,
    )(*args)


def step(
    obs_count,
    obs_point,
    obs_frame,
    jac_cam,
    jac_point,
    residual,
    point_inv,
    band,
    edge_weight,
    precond,
):
    slots = obs_point.shape[0]
    pid = obs_point.reshape(1, slots)
    fid = obs_frame.reshape(1, slots)
    count = lax.axis_size("frames")
    edge = edge_weight.reshape(1, FR)
    bands = jnp.transpose(band, (1, 2, 0, 3))

    far = plain(
        grad_kernel,
        [sds(Q, PT)] * (GROUPS - 1),
        (obs_count, pid, residual, jac_point),
        raw=(0, 1, 2, 3),
        scratch=[
            pltpu.SMEM((GROUPS,), jnp.int32),
            pltpu.VMEM((1, slots), jnp.int32),
            pltpu.VMEM((2, slots), F32),
            pltpu.VMEM((GROUPS - 1, 2, Q, CAP), F32),
            pltpu.SemaphoreType.DMA((GROUPS + 2,)),
        ],
        est=cost(2 * 192 * 256 * 6144, 2 * 24 * 6144 * 4),
    )
    ints = jax.ShapeDtypeStruct((1, slots), jnp.int32)
    near, pid, fid = plain(
        own_kernel,
        [sds(Q, PT), ints, ints],
        (far[0], obs_count, pid, fid, residual, jac_point),
        raw=(1, 2, 3, 4, 5),
        scratch=[
            pltpu.SMEM((GROUPS,), jnp.int32),
            pltpu.VMEM((2, CAP), F32),
            pltpu.VMEM((2, Q, CAP), F32),
            pltpu.SemaphoreType.DMA((5,)),
        ],
        est=cost(2 * 192 * 256 * 2048, 2 * 24 * 2048 * 4),
    )
    got = [shifted(far[GROUPS - 1 - s], "points", s) for s in (3, 2, 1)] + [near]
    solved = plain(
        solve_kernel, sds(Q, PT), (*got, point_inv), est=cost(2 * Q * Q * PT, Q * Q * PT * 4)
    )
    partial = ()
    for s in (0, 1, 3, 2):
        piece = shifted(solved, "points", s) if s else solved
        partial = (
            plain(
                functools.partial(rhs_kernel, -s),
                sds(CP, FR),
                (pid, fid, residual, jac_point, jac_cam, *partial, piece),
                est=cost(2 * 256 * 256 * 2048, 2 * 32 * 2048 * 4),
            ),
        )
    (partial,) = partial
    parts = [partial] + [shifted(partial, "points", s) for s in (1, 2, 3)]

    rhs, z = plain(
        start_kernel, [sds(CP, FR), sds(8, FR)], (*parts, precond, edge), est=cost(20000, 100000)
    )
    z_left, z_right = beside(z)
    w, u = plain(
        first_kernel,
        [sds(CP, FR), sds(8, FR)],
        (z, z_left, z_right, bands, precond),
        est=cost(2 * 127 * 36 * 256, 127 * 36 * 256 * 4),
    )
    u_right = lax.ppermute(u, "frames", [(i + 1, i) for i in range(count - 1)])
    back = plain(
        back_kernel,
        [sds(2 * Q, PT)] * GROUPS,
        (pid, fid, jac_point, jac_cam, z, u),
        est=cost(2 * 400 * 256 * 8192, 2 * 32 * 8192 * 4),
    )
    returned = [shifted(back[GROUPS - 1 - s], "points", s) for s in (3, 2, 1)] + [back[GROUPS - 1]]
    gram = plain(
        second_kernel,
        sds(count, 128),
        (u, u_right, bands, rhs, z, w),
        est=cost(127 * 36 * 256, 127 * 18 * 256 * 4),
    )
    gram = lax.all_to_all(gram, "frames", split_axis=0, concat_axis=0, tiled=True)
    undo_z, undo_u = plain(
        undo_kernel,
        [sds(Q, PT)] * 2,
        (*returned, point_inv),
        raw=(4,),
        scratch=[pltpu.VMEM((Q, Q, PT), F32), pltpu.SemaphoreType.DMA],
        est=cost(4 * Q * Q * PT, Q * Q * PT * 4),
    )
    camera_step, point_step = plain(
        final_kernel,
        [sds(CP, FR), sds(Q, PT)],
        (gram, z, u, solved, undo_z, undo_u),
        est=cost(6 * Q * PT, 6 * Q * PT * 4),
    )
    return camera_step, point_step


def solution(mesh):
    placed = (
        P(("frames", "points")),
        P(("frames", "points")),
        P(("frames", "points")),
        P(None, None, ("frames", "points")),
        P(None, None, ("frames", "points")),
        P(None, ("frames", "points")),
        P(None, None, ("frames", "points")),
        P(None, None, None, "frames"),
        P("frames"),
        P(None, None, "frames"),
    )
    return jax.shard_map(
        step,
        mesh=mesh,
        in_specs=placed,
        out_specs=(P(None, "frames"), P(None, ("frames", "points"))),
        check_vma=False,
    )
```

```python
import functools

import jax
import jax.numpy as jnp
from jax import lax
from jax.experimental import pallas as pl
from jax.experimental.pallas import tpu as pltpu
from jax.sharding import PartitionSpec as P


F32 = jnp.float32
BF16 = jnp.bfloat16
CP = 6
Q = 24
BANDW = 127
REACH = 63
FR = 256
PT = 1024
CAP = 2048
GROUPS = 4
LO = 256
HI = PT // LO
LIMIT = pltpu.CompilerParams(vmem_limit_bytes=12 * 2**20)


def halves(x):
    lead = x.astype(BF16).astype(F32)
    return jnp.concatenate([lead, x - lead], axis=0).astype(BF16)


def one_hot(row, rows):
    n = row.shape[1]
    index = lax.broadcasted_iota(jnp.int32, (rows, 128), 0).astype(F32).astype(BF16)
    row = row.astype(BF16)
    cols = []
    for c in range(n // 128):
        here = jnp.broadcast_to(row[:, c * 128 : (c + 1) * 128], (rows, 128))
        cols.append(jnp.where(index == here, jnp.ones_like(index), jnp.zeros_like(index)))
    return jnp.concatenate(cols, axis=1)


def split_ids(ids):
    hi = lax.shift_right_logical(ids, 8)
    lo = lax.bitwise_and(ids, LO - 1)
    return hi.astype(F32), lo.astype(F32)


def used_or(ids, count, other):
    lane = lax.broadcasted_iota(jnp.int32, ids.shape, 1)
    return jnp.where(lane < count, ids, other)


def scatter_points(terms, ids):
    n = terms.shape[0]
    hi, lo = split_ids(ids)
    parts = halves(terms)
    table = one_hot(lo, LO)
    rows = []
    for h in range(HI):
        mask = jnp.broadcast_to((hi == h).astype(F32), (2 * n, CAP)).astype(BF16)
        rows.append(parts * mask)
    sums = lax.dot_general(
        jnp.concatenate(rows, axis=0), table, (((1,), (1,)), ((), ())), preferred_element_type=F32
    )
    out = []
    for h in range(HI):
        block = sums[h * 2 * n : (h + 1) * 2 * n]
        out.append(block[:n] + block[n:])
    return jnp.concatenate(out, axis=1)


def gather_points(values, ids):
    n = values.shape[0]
    hi, lo = split_ids(ids)
    parts = halves(values)
    table = one_hot(lo, LO)
    stacked = jnp.concatenate([parts[:, h * LO : (h + 1) * LO] for h in range(HI)], axis=0)
    got = lax.dot_general(stacked, table, (((1,), (0,)), ((), ())), preferred_element_type=F32)
    total = None
    for h in range(HI):
        block = got[h * 2 * n : (h + 1) * 2 * n]
        term = (block[:n] + block[n:]) * (hi == h).astype(F32)
        total = term if total is None else total + term
    return total


def block_at(turn):
    return lax.bitwise_xor(lax.axis_index("points"), abs(turn))


def lanes(b):
    return pl.ds(pl.multiple_of(b * CAP, CAP), CAP)


def fetch(pairs, sems):
    copies = [pltpu.make_async_copy(src, dst, sems.at[i]) for i, (src, dst) in enumerate(pairs)]
    for copy in copies:
        copy.start()
    return copies


def sums_toward(b, ids_ref, res_ref, jp_ref):
    at = lanes(b)
    terms = jp_ref[0, :, at] * res_ref[0:1, at] + jp_ref[1, :, at] * res_ref[1:2, at]
    return scatter_points(terms, ids_ref[:, at])


def load_kernel(
    count_hbm, pid_hbm, fid_hbm, res_hbm, jp_hbm, out_ref, pid_ref, fid_ref, res_ref, jp_ref, count_ref, sems
):
    small = [(count_hbm, count_ref), (pid_hbm, pid_ref), (res_hbm, res_ref), (fid_hbm, fid_ref)]
    blocks = [block_at(turn) for turn in (2, 1, 3, 0)]
    large = [(jp_hbm.at[:, :, lanes(b)], jp_ref.at[:, :, lanes(b)]) for b in blocks]
    copies = fetch(small[:3] + large[:1] + small[3:] + large[1:], sems)
    for copy in copies[:3]:
        copy.wait()
    for g in range(GROUPS):
        here = slice(g * CAP, (g + 1) * CAP)
        pid_ref[:, here] = used_or(pid_ref[:, here], count_ref[g], PT)
    copies[3].wait()
    out_ref[...] = sums_toward(blocks[0], pid_ref, res_ref, jp_ref)
    copies[4].wait()
    for g in range(GROUPS):
        here = slice(g * CAP, (g + 1) * CAP)
        fid_ref[:, here] = used_or(fid_ref[:, here], count_ref[g], FR)
    for copy in copies[5:]:
        copy.wait()


def grad_kernel(turns, ids_ref, res_ref, jp_ref, *outs):
    for turn, out_ref in zip(turns, outs):
        out_ref[...] = sums_toward(block_at(turn), ids_ref, res_ref, jp_ref)


def solve_kernel(a_ref, b_ref, c_ref, d_ref, inv_ref, out_ref):
    grad = a_ref[...] + b_ref[...] + c_ref[...] + d_ref[...]
    out_ref[...] = jnp.sum(inv_ref[...] * grad[None], axis=1)


def rhs_kernel(turn, pid_ref, fid_ref, res_ref, jp_ref, jc_ref, *rest):
    solved_ref, out_ref = rest[-2:]
    b = block_at(turn)
    at = lanes(b)
    seen = gather_points(solved_ref[...], pid_ref[:, at])
    remain = [
        res_ref[a : a + 1, at] - jnp.sum(jp_ref[a, :, at] * seen, axis=0, keepdims=True)
        for a in range(2)
    ]
    cam = jc_ref[0, :, at] * remain[0] + jc_ref[1, :, at] * remain[1]
    cam = jnp.concatenate([cam, jnp.zeros((2, CAP), F32)], axis=0)
    table = one_hot(fid_ref[:, at].astype(F32), FR)
    sums = lax.dot_general(
        halves(cam), table, (((1,), (1,)), ((), ())), preferred_element_type=F32
    )
    total = sums[0:CP] + sums[8 : 8 + CP]
    out_ref[...] = total if len(rest) == 2 else total + rest[0][...]


def apply_precond(pre_ref, vec):
    return jnp.sum(pre_ref[...] * vec[None], axis=1)


def start_kernel(a_ref, b_ref, c_ref, d_ref, pre_ref, edge_ref, r_ref, z_ref):
    rhs = a_ref[...] + b_ref[...] + c_ref[...] + d_ref[...]
    r_ref[...] = rhs
    lane = lax.broadcasted_iota(jnp.int32, (1, FR), 1)
    last = lax.axis_index("frames") == lax.axis_size("frames") - 1
    edge = edge_ref[...] * jnp.where((lane == FR - 1) & last, 0.0, 1.0)
    z = apply_precond(pre_ref, rhs)
    z_ref[...] = jnp.concatenate([z, edge, jnp.zeros((1, FR), F32)], axis=0)


def steps_of(row):
    n = row.shape[1]
    sub = lax.broadcasted_iota(jnp.int32, (8, n), 0)
    x = jnp.broadcast_to(row, (8, n))
    for bit in (1, 2, 4):
        x = jnp.where((sub & bit) != 0, pltpu.roll(x, n - bit, 1), x)
    return x


def banded_sums(band_ref, rows, tiles, first=None):
    totals = [None] * CP
    ends = [None] * CP
    for j in range(CP):
        stepped = steps_of(rows[j])
        for t in tiles:
            at = 128 - REACH + 8 * t
            shifted = stepped[:, at : at + FR]
            if t == first:
                sub = lax.broadcasted_iota(jnp.int32, (8, FR), 0)
                shifted = jnp.where(sub == 7, 0.5 * shifted, 0.0)
            for i in range(CP):
                if 8 * t + 8 <= BANDW:
                    term = band_ref[i, j, 8 * t : 8 * t + 8, :] * shifted
                    totals[i] = term if totals[i] is None else totals[i] + term
                else:
                    count = BANDW - 8 * t
                    term = band_ref[i, j, 8 * t : BANDW, :] * shifted[:count]
                    ends[i] = term if ends[i] is None else ends[i] + term
    return jnp.concatenate(
        [
            jnp.sum(t, axis=0, keepdims=True) + jnp.sum(e, axis=0, keepdims=True)
            for t, e in zip(totals, ends)
        ],
        axis=0,
    )


def first_kernel(z_ref, outer_ref, inner_ref, band_ref, pre_ref, w_ref, u_ref):
    even = lax.rem(lax.axis_index("frames"), 2) == 0
    sides = (outer_ref[...], inner_ref[...])
    left = jnp.where(even, sides[0], sides[1])
    right = jnp.where(even, sides[1], sides[0])
    padded = jnp.concatenate([left, z_ref[...], right], axis=1)
    near = padded[:, FR - 128 : 2 * FR + 128]
    banded = banded_sums(band_ref, [near[j : j + 1] for j in range(CP)], range(16))
    own = z_ref[:CP, :]
    here = z_ref[CP : CP + 1, :]
    prev = padded[CP : CP + 1, FR - 1 : 2 * FR - 1]
    before = padded[:CP, FR - 1 : 2 * FR - 1]
    after = padded[:CP, FR + 1 : 2 * FR + 1]
    image = banded + prev * (own - before) + here * (own - after)
    w_ref[...] = image
    u = apply_precond(pre_ref, image)
    u_ref[...] = jnp.concatenate([u, jnp.zeros((2, FR), F32)], axis=0)


def second_kernel(u_ref, right_ref, band_ref, r_ref, z_ref, w_ref, out_ref):
    ahead = jnp.concatenate([u_ref[...], right_ref[...]], axis=1)
    near = jnp.concatenate([jnp.zeros((8, 128), F32), ahead[:, : FR + 128]], axis=1)
    upper = banded_sums(band_ref, [near[j : j + 1] for j in range(CP)], range(7, 16), first=7)
    u, z, w, r = u_ref[:CP, :], z_ref[:CP, :], w_ref[...], r_ref[...]
    edge = z_ref[CP : CP + 1, :]
    step = u - ahead[:CP, 1 : FR + 1]
    lane = lax.broadcasted_iota(jnp.int32, (1, 128), 1)
    row = jnp.zeros((1, 128), F32)
    for at, term in enumerate((r * z, z * w, w * u, 2.0 * u * upper + edge * step * step)):
        total = jnp.sum(jnp.sum(term, axis=0, keepdims=True), axis=1, keepdims=True)
        row = row + jnp.where(lane == at, total, 0.0)
    out_ref[...] = jnp.broadcast_to(row, out_ref.shape)


def back_kernel(pid_ref, fid_ref, jp_ref, jc_ref, z_ref, u_ref, *outs):
    parts = halves(jnp.concatenate([z_ref[...], u_ref[...]], axis=0))
    for j in range(GROUPS):
        b = block_at(GROUPS - 1 - j)
        at = lanes(b)
        table = one_hot(fid_ref[:, at].astype(F32), FR)
        got = lax.dot_general(parts, table, (((1,), (0,)), ((), ())), preferred_element_type=F32)
        got = got[:16] + got[16:]
        terms = []
        for v in range(2):
            seen = got[v * 8 : v * 8 + CP]
            pair = [jnp.sum(jc_ref[a, :, at] * seen, axis=0, keepdims=True) for a in range(2)]
            terms.append(jp_ref[0, :, at] * pair[0] + jp_ref[1, :, at] * pair[1])
        outs[j][...] = scatter_points(jnp.concatenate(terms, axis=0), pid_ref[:, at])


def undo_kernel(a_ref, b_ref, c_ref, d_ref, inv_hbm, z_ref, u_ref, inv_ref, sem):
    pltpu.async_copy(inv_hbm, inv_ref, sem).wait()
    both = a_ref[...] + b_ref[...] + c_ref[...] + d_ref[...]
    z_ref[...] = jnp.sum(inv_ref[...] * both[None, :Q], axis=1)
    u_ref[...] = jnp.sum(inv_ref[...] * both[None, Q:], axis=1)


def final_kernel(g_ref, z_ref, u_ref, ps_ref, pz_ref, pu_ref, cam_ref, pt_ref):
    row = jnp.sum(g_ref[...], axis=0, keepdims=True)
    rz, zw, wu, uy = [row[:, i : i + 1] for i in range(4)]
    a0 = rz / zw
    inner = a0 * a0 * wu - rz
    beta = 1.0 + inner / rz
    curve = beta * beta * zw - 2.0 * beta * a0 * wu + a0 * a0 * uy
    a1 = inner / curve
    c0 = a0 + a1 * beta
    c1 = -a1 * a0
    cam_ref[...] = c0 * z_ref[:CP, :] + c1 * u_ref[:CP, :]
    pt_ref[...] = ps_ref[...] - c0 * pz_ref[...] - c1 * pu_ref[...]


def shifted(value, axis, turn):
    return lax.ppermute(value, axis, [(i, i ^ turn) for i in range(GROUPS)])


def beside(value):
    count = lax.axis_size("frames")
    inner = [(i, i ^ 1) for i in range(count)]
    outer = [pair for i in range(1, count - 1, 2) for pair in ((i, i + 1), (i + 1, i))]
    far = lax.ppermute(value, "frames", outer)
    near = lax.ppermute(value, "frames", inner)
    return far, near


def sds(*shape):
    return jax.ShapeDtypeStruct(shape, F32)


def cost(flops, moved):
    return pl.CostEstimate(flops=flops, bytes_accessed=moved, transcendentals=0)


def plain(kernel, outs, args, smem=(), raw=(), scratch=(), est=None, ):
    space = lambda i: pltpu.SMEM if i in smem else pltpu.HBM if i in raw else pltpu.VMEM
    specs = [pl.BlockSpec(memory_space=space(i)) for i in range(len(args))]
    args = [pltpu.with_memory_space_constraint(x, pltpu.HBM) if i in raw else x for i, x in enumerate(args)]
    out_specs = jax.tree.map(lambda _: pl.BlockSpec(memory_space=pltpu.VMEM), outs)
    return pl.pallas_call(
        kernel,
        in_specs=specs,
        out_specs=out_specs,
        out_shape=outs,
        scratch_shapes=list(scratch),
        cost_estimate=est,
        compiler_params=LIMIT,
    )(*args)


def step(
    obs_count,
    obs_point,
    obs_frame,
    jac_cam,
    jac_point,
    residual,
    point_inv,
    band,
    edge_weight,
    precond,
):
    slots = obs_point.shape[0]
    pid = obs_point.reshape(1, slots)
    fid = obs_frame.reshape(1, slots)
    count = lax.axis_size("frames")
    edge = edge_weight.reshape(1, FR)
    bands = jnp.transpose(band, (1, 2, 0, 3))

    ints = jax.ShapeDtypeStruct((1, slots), jnp.int32)
    far, pid, fid, res, jac = plain(
        load_kernel,
        [sds(Q, PT), ints, ints, sds(2, slots), sds(2, Q, slots)],
        (obs_count, pid, fid, residual, jac_point),
        raw=(0, 1, 2, 3, 4),
        scratch=[pltpu.SMEM((GROUPS,), jnp.int32), pltpu.SemaphoreType.DMA((8,))],
        est=cost(2 * 192 * 256 * 2048, 2 * 24 * 8192 * 4),
    )
    grad = lambda *turns: plain(
        functools.partial(grad_kernel, turns),
        [sds(Q, PT)] * len(turns),
        (pid, res, jac),
        est=cost(2 * 192 * 256 * 2048 * len(turns), 2 * 24 * 2048 * 4 * len(turns)),
    )
    got = []
    for turn, sums in zip((2, 1, 3), [far, *grad(1, 3)]):
        got.append(shifted(sums, "points", turn))
    got.extend(grad(0))
    solved = plain(
        solve_kernel, sds(Q, PT), (*got, point_inv), est=cost(2 * Q * Q * PT, Q * Q * PT * 4)
    )
    partial = ()
    for s in (0, 1, 3, 2):
        piece = shifted(solved, "points", s) if s else solved
        partial = (
            plain(
                functools.partial(rhs_kernel, -s),
                sds(CP, FR),
                (pid, fid, res, jac, jac_cam, *partial, piece),
                est=cost(2 * 256 * 256 * 2048, 2 * 32 * 2048 * 4),
            ),
        )
    (partial,) = partial
    parts = [partial]
    for s in (1, 2, 3):
        parts.append(shifted(partial, "points", s))

    rhs, z = plain(
        start_kernel, [sds(CP, FR), sds(8, FR)], (*parts, precond, edge), est=cost(20000, 100000)
    )
    z_left, z_right = beside(z)
    w, u = plain(
        first_kernel,
        [sds(CP, FR), sds(8, FR)],
        (z, z_left, z_right, bands, precond),
        est=cost(2 * 127 * 36 * 256, 127 * 36 * 256 * 4),
    )
    u_right = lax.ppermute(u, "frames", [(i + 1, i) for i in range(count - 1)])
    back = plain(
        back_kernel,
        [sds(2 * Q, PT)] * GROUPS,
        (pid, fid, jac, jac_cam, z, u),
        est=cost(2 * 400 * 256 * 8192, 2 * 32 * 8192 * 4),
    )
    returned = [back[GROUPS - 1]]
    for s in (3, 2, 1):
        returned.append(shifted(back[GROUPS - 1 - s], "points", s))
    gram = plain(
        second_kernel,
        sds(count, 128),
        (u, u_right, bands, rhs, z, w),
        est=cost(127 * 36 * 256, 127 * 18 * 256 * 4),
    )
    gram = lax.all_to_all(gram, "frames", split_axis=0, concat_axis=0, tiled=True)
    undo_z, undo_u = plain(
        undo_kernel,
        [sds(Q, PT)] * 2,
        (*returned, point_inv),
        raw=(4,),
        scratch=[pltpu.VMEM((Q, Q, PT), F32), pltpu.SemaphoreType.DMA],
        est=cost(4 * Q * Q * PT, Q * Q * PT * 4),
    )
    camera_step, point_step = plain(
        final_kernel,
        [sds(CP, FR), sds(Q, PT)],
        (gram, z, u, solved, undo_z, undo_u),
        est=cost(6 * Q * PT, 6 * Q * PT * 4),
    )
    return camera_step, point_step


def solution(mesh):
    placed = (
        P(("frames", "points")),
        P(("frames", "points")),
        P(("frames", "points")),
        P(None, None, ("frames", "points")),
        P(None, None, ("frames", "points")),
        P(None, ("frames", "points")),
        P(None, None, ("frames", "points")),
        P(None, None, None, "frames"),
        P("frames"),
        P(None, None, "frames"),
    )
    return jax.shard_map(
        step,
        mesh=mesh,
        in_specs=placed,
        out_specs=(P(None, "frames"), P(None, ("frames", "points"))),
        check_vma=False,
    )
```

```python
import functools

import jax
import jax.numpy as jnp
from jax import lax
from jax.experimental import pallas as pl
from jax.experimental.pallas import tpu as pltpu
from jax.sharding import PartitionSpec as P


F32 = jnp.float32
BF16 = jnp.bfloat16
CP = 6
Q = 24
BANDW = 127
REACH = 63
FR = 256
PT = 1024
CAP = 2048
GROUPS = 4
LO = 256
HI = PT // LO
SUM_TURNS = ((2, 2), (1, 3), (3, 1))
SOLVED_TURNS = ((3, 1), (1, 3), (2, 2))
CAMERA_TURNS = ((3, 1), (2, 2), (1, 3))
SELF = ((0, 0),)
LIMIT = pltpu.CompilerParams(vmem_limit_bytes=12 * 2**20)


def halves(x):
    lead = x.astype(BF16).astype(F32)
    return jnp.concatenate([lead, x - lead], axis=0).astype(BF16)


def one_hot(row, rows):
    n = row.shape[1]
    index = lax.broadcasted_iota(jnp.int32, (rows, 128), 0).astype(F32).astype(BF16)
    row = row.astype(BF16)
    cols = []
    for c in range(n // 128):
        here = jnp.broadcast_to(row[:, c * 128 : (c + 1) * 128], (rows, 128))
        cols.append(jnp.where(index == here, jnp.ones_like(index), jnp.zeros_like(index)))
    return jnp.concatenate(cols, axis=1)


def split_ids(ids):
    hi = lax.shift_right_logical(ids, 8)
    lo = lax.bitwise_and(ids, LO - 1)
    return hi.astype(F32), lo.astype(F32)


def used_or(ids, count, other):
    lane = lax.broadcasted_iota(jnp.int32, ids.shape, 1)
    return jnp.where(lane < count, ids, other)


def scatter_points(terms, ids):
    n = terms.shape[0]
    hi, lo = split_ids(ids)
    parts = halves(terms)
    table = one_hot(lo, LO)
    rows = []
    for h in range(HI):
        mask = jnp.broadcast_to((hi == h).astype(F32), (2 * n, CAP)).astype(BF16)
        rows.append(parts * mask)
    sums = lax.dot_general(
        jnp.concatenate(rows, axis=0), table, (((1,), (1,)), ((), ())), preferred_element_type=F32
    )
    out = []
    for h in range(HI):
        block = sums[h * 2 * n : (h + 1) * 2 * n]
        out.append(block[:n] + block[n:])
    return jnp.concatenate(out, axis=1)


def gather_points(values, ids):
    n = values.shape[0]
    hi, lo = split_ids(ids)
    parts = halves(values)
    table = one_hot(lo, LO)
    stacked = jnp.concatenate([parts[:, h * LO : (h + 1) * LO] for h in range(HI)], axis=0)
    got = lax.dot_general(stacked, table, (((1,), (0,)), ((), ())), preferred_element_type=F32)
    total = None
    for h in range(HI):
        block = got[h * 2 * n : (h + 1) * 2 * n]
        term = (block[:n] + block[n:]) * (hi == h).astype(F32)
        total = term if total is None else total + term
    return total


def block_at(turn):
    first = lax.rem(lax.axis_index("frames"), 2) == 0
    return lax.bitwise_xor(lax.axis_index("points"), jnp.where(first, turn[0], turn[1]))


def lanes(b):
    return pl.ds(pl.multiple_of(b * CAP, CAP), CAP)


def fetch(pairs, sems):
    copies = [pltpu.make_async_copy(src, dst, sems.at[i]) for i, (src, dst) in enumerate(pairs)]
    for copy in copies:
        copy.start()
    return copies


def sums_toward(b, ids_ref, res_ref, jp_ref):
    at = lanes(b)
    terms = jp_ref[0, :, at] * res_ref[0:1, at] + jp_ref[1, :, at] * res_ref[1:2, at]
    return scatter_points(terms, ids_ref[:, at])


def load_kernel(
    count_hbm, pid_hbm, fid_hbm, res_hbm, jp_hbm, out_ref, pid_ref, fid_ref, res_ref, jp_ref, count_ref, sems
):
    small = [(count_hbm, count_ref), (pid_hbm, pid_ref), (res_hbm, res_ref), (fid_hbm, fid_ref)]
    blocks = [block_at(turn) for turn in SUM_TURNS + SELF]
    large = [(jp_hbm.at[:, :, lanes(b)], jp_ref.at[:, :, lanes(b)]) for b in blocks]
    copies = fetch(small[:3] + large[:1] + small[3:] + large[1:], sems)
    for copy in copies[:3]:
        copy.wait()
    for g in range(GROUPS):
        here = slice(g * CAP, (g + 1) * CAP)
        pid_ref[:, here] = used_or(pid_ref[:, here], count_ref[g], PT)
    copies[3].wait()
    out_ref[...] = sums_toward(blocks[0], pid_ref, res_ref, jp_ref)
    copies[4].wait()
    for g in range(GROUPS):
        here = slice(g * CAP, (g + 1) * CAP)
        fid_ref[:, here] = used_or(fid_ref[:, here], count_ref[g], FR)
    for copy in copies[5:]:
        copy.wait()


def grad_kernel(turns, ids_ref, res_ref, jp_ref, *outs):
    for turn, out_ref in zip(turns, outs):
        out_ref[...] = sums_toward(block_at(turn), ids_ref, res_ref, jp_ref)


def solve_kernel(a_ref, b_ref, c_ref, d_ref, inv_ref, out_ref):
    grad = a_ref[...] + b_ref[...] + c_ref[...] + d_ref[...]
    out_ref[...] = jnp.sum(inv_ref[...] * grad[None], axis=1)


def rhs_kernel(turn, pid_ref, fid_ref, res_ref, jp_ref, jc_ref, *rest):
    solved_ref, out_ref = rest[-2:]
    b = block_at(turn)
    at = lanes(b)
    seen = gather_points(solved_ref[...], pid_ref[:, at])
    remain = [
        res_ref[a : a + 1, at] - jnp.sum(jp_ref[a, :, at] * seen, axis=0, keepdims=True)
        for a in range(2)
    ]
    cam = jc_ref[0, :, at] * remain[0] + jc_ref[1, :, at] * remain[1]
    cam = jnp.concatenate([cam, jnp.zeros((2, CAP), F32)], axis=0)
    table = one_hot(fid_ref[:, at].astype(F32), FR)
    sums = lax.dot_general(
        halves(cam), table, (((1,), (1,)), ((), ())), preferred_element_type=F32
    )
    total = sums[0:CP] + sums[8 : 8 + CP]
    out_ref[...] = total if len(rest) == 2 else total + rest[0][...]


def apply_precond(pre_ref, vec):
    return jnp.sum(pre_ref[...] * vec[None], axis=1)


def start_kernel(a_ref, b_ref, c_ref, d_ref, pre_ref, edge_ref, r_ref, z_ref):
    rhs = a_ref[...] + b_ref[...] + c_ref[...] + d_ref[...]
    r_ref[...] = rhs
    lane = lax.broadcasted_iota(jnp.int32, (1, FR), 1)
    last = lax.axis_index("frames") == lax.axis_size("frames") - 1
    edge = edge_ref[...] * jnp.where((lane == FR - 1) & last, 0.0, 1.0)
    z = apply_precond(pre_ref, rhs)
    z_ref[...] = jnp.concatenate([z, edge, jnp.zeros((1, FR), F32)], axis=0)


def steps_of(row):
    n = row.shape[1]
    sub = lax.broadcasted_iota(jnp.int32, (8, n), 0)
    x = jnp.broadcast_to(row, (8, n))
    for bit in (1, 2, 4):
        x = jnp.where((sub & bit) != 0, pltpu.roll(x, n - bit, 1), x)
    return x


def banded_sums(band_ref, rows, tiles, first=None):
    totals = [None] * CP
    ends = [None] * CP
    for j in range(CP):
        stepped = steps_of(rows[j])
        for t in tiles:
            at = 128 - REACH + 8 * t
            shifted = stepped[:, at : at + FR]
            if t == first:
                sub = lax.broadcasted_iota(jnp.int32, (8, FR), 0)
                shifted = jnp.where(sub == 7, 0.5 * shifted, 0.0)
            for i in range(CP):
                if 8 * t + 8 <= BANDW:
                    term = band_ref[i, j, 8 * t : 8 * t + 8, :] * shifted
                    totals[i] = term if totals[i] is None else totals[i] + term
                else:
                    count = BANDW - 8 * t
                    term = band_ref[i, j, 8 * t : BANDW, :] * shifted[:count]
                    ends[i] = term if ends[i] is None else ends[i] + term
    return jnp.concatenate(
        [
            jnp.sum(t, axis=0, keepdims=True) + jnp.sum(e, axis=0, keepdims=True)
            for t, e in zip(totals, ends)
        ],
        axis=0,
    )


def first_kernel(z_ref, outer_ref, inner_ref, band_ref, pre_ref, w_ref, u_ref):
    even = lax.rem(lax.axis_index("frames"), 2) == 0
    sides = (outer_ref[...], inner_ref[...])
    left = jnp.where(even, sides[0], sides[1])
    right = jnp.where(even, sides[1], sides[0])
    padded = jnp.concatenate([left, z_ref[...], right], axis=1)
    near = padded[:, FR - 128 : 2 * FR + 128]
    banded = banded_sums(band_ref, [near[j : j + 1] for j in range(CP)], range(16))
    own = z_ref[:CP, :]
    here = z_ref[CP : CP + 1, :]
    prev = padded[CP : CP + 1, FR - 1 : 2 * FR - 1]
    before = padded[:CP, FR - 1 : 2 * FR - 1]
    after = padded[:CP, FR + 1 : 2 * FR + 1]
    image = banded + prev * (own - before) + here * (own - after)
    w_ref[...] = image
    u = apply_precond(pre_ref, image)
    u_ref[...] = jnp.concatenate([u, jnp.zeros((2, FR), F32)], axis=0)


def second_kernel(u_ref, right_ref, band_ref, r_ref, z_ref, w_ref, out_ref):
    ahead = jnp.concatenate([u_ref[...], right_ref[...]], axis=1)
    near = jnp.concatenate([jnp.zeros((8, 128), F32), ahead[:, : FR + 128]], axis=1)
    upper = banded_sums(band_ref, [near[j : j + 1] for j in range(CP)], range(7, 16), first=7)
    u, z, w, r = u_ref[:CP, :], z_ref[:CP, :], w_ref[...], r_ref[...]
    edge = z_ref[CP : CP + 1, :]
    step = u - ahead[:CP, 1 : FR + 1]
    lane = lax.broadcasted_iota(jnp.int32, (1, 128), 1)
    row = jnp.zeros((1, 128), F32)
    for at, term in enumerate((r * z, z * w, w * u, 2.0 * u * upper + edge * step * step)):
        total = jnp.sum(jnp.sum(term, axis=0, keepdims=True), axis=1, keepdims=True)
        row = row + jnp.where(lane == at, total, 0.0)
    out_ref[...] = jnp.broadcast_to(row, out_ref.shape)


def back_kernel(pid_ref, fid_ref, jp_ref, jc_ref, z_ref, u_ref, *outs):
    parts = halves(jnp.concatenate([z_ref[...], u_ref[...]], axis=0))
    for j in range(GROUPS):
        b = block_at((GROUPS - 1 - j,) * 2)
        at = lanes(b)
        table = one_hot(fid_ref[:, at].astype(F32), FR)
        got = lax.dot_general(parts, table, (((1,), (0,)), ((), ())), preferred_element_type=F32)
        got = got[:16] + got[16:]
        terms = []
        for v in range(2):
            seen = got[v * 8 : v * 8 + CP]
            pair = [jnp.sum(jc_ref[a, :, at] * seen, axis=0, keepdims=True) for a in range(2)]
            terms.append(jp_ref[0, :, at] * pair[0] + jp_ref[1, :, at] * pair[1])
        outs[j][...] = scatter_points(jnp.concatenate(terms, axis=0), pid_ref[:, at])


def undo_kernel(a_ref, b_ref, c_ref, d_ref, inv_hbm, z_ref, u_ref, inv_ref, sem):
    pltpu.async_copy(inv_hbm, inv_ref, sem).wait()
    both = a_ref[...] + b_ref[...] + c_ref[...] + d_ref[...]
    z_ref[...] = jnp.sum(inv_ref[...] * both[None, :Q], axis=1)
    u_ref[...] = jnp.sum(inv_ref[...] * both[None, Q:], axis=1)


def final_kernel(g_ref, z_ref, u_ref, ps_ref, pz_ref, pu_ref, cam_ref, pt_ref):
    row = jnp.sum(g_ref[...], axis=0, keepdims=True)
    rz, zw, wu, uy = [row[:, i : i + 1] for i in range(4)]
    a0 = rz / zw
    inner = a0 * a0 * wu - rz
    beta = 1.0 + inner / rz
    curve = beta * beta * zw - 2.0 * beta * a0 * wu + a0 * a0 * uy
    a1 = inner / curve
    c0 = a0 + a1 * beta
    c1 = -a1 * a0
    cam_ref[...] = c0 * z_ref[:CP, :] + c1 * u_ref[:CP, :]
    pt_ref[...] = ps_ref[...] - c0 * pz_ref[...] - c1 * pu_ref[...]


def swapped(value, turn):
    pairs = [
        (GROUPS * f + p, GROUPS * f + (p ^ turn[f % 2]))
        for f in range(lax.axis_size("frames"))
        for p in range(GROUPS)
    ]
    return lax.ppermute(value, ("frames", "points"), pairs)


def beside(value):
    count = lax.axis_size("frames")
    inner = [(i, i ^ 1) for i in range(count)]
    outer = [pair for i in range(1, count - 1, 2) for pair in ((i, i + 1), (i + 1, i))]
    far = lax.ppermute(value, "frames", outer)
    near = lax.ppermute(value, "frames", inner)
    return far, near


def sds(*shape):
    return jax.ShapeDtypeStruct(shape, F32)


def cost(flops, moved):
    return pl.CostEstimate(flops=flops, bytes_accessed=moved, transcendentals=0)


def plain(kernel, outs, args, smem=(), raw=(), scratch=(), est=None, ):
    space = lambda i: pltpu.SMEM if i in smem else pltpu.HBM if i in raw else pltpu.VMEM
    specs = [pl.BlockSpec(memory_space=space(i)) for i in range(len(args))]
    args = [pltpu.with_memory_space_constraint(x, pltpu.HBM) if i in raw else x for i, x in enumerate(args)]
    out_specs = jax.tree.map(lambda _: pl.BlockSpec(memory_space=pltpu.VMEM), outs)
    return pl.pallas_call(
        kernel,
        in_specs=specs,
        out_specs=out_specs,
        out_shape=outs,
        scratch_shapes=list(scratch),
        cost_estimate=est,
        compiler_params=LIMIT,
    )(*args)


def step(
    obs_count,
    obs_point,
    obs_frame,
    jac_cam,
    jac_point,
    residual,
    point_inv,
    band,
    edge_weight,
    precond,
):
    slots = obs_point.shape[0]
    pid = obs_point.reshape(1, slots)
    fid = obs_frame.reshape(1, slots)
    count = lax.axis_size("frames")
    edge = edge_weight.reshape(1, FR)
    bands = jnp.transpose(band, (1, 2, 0, 3))

    ints = jax.ShapeDtypeStruct((1, slots), jnp.int32)
    far, pid, fid, res, jac = plain(
        load_kernel,
        [sds(Q, PT), ints, ints, sds(2, slots), sds(2, Q, slots)],
        (obs_count, pid, fid, residual, jac_point),
        raw=(0, 1, 2, 3, 4),
        scratch=[pltpu.SMEM((GROUPS,), jnp.int32), pltpu.SemaphoreType.DMA((8,))],
        est=cost(2 * 192 * 256 * 2048, 2 * 24 * 8192 * 4),
    )
    grad = lambda *turns: plain(
        functools.partial(grad_kernel, turns),
        [sds(Q, PT)] * len(turns),
        (pid, res, jac),
        est=cost(2 * 192 * 256 * 2048 * len(turns), 2 * 24 * 2048 * 4 * len(turns)),
    )
    got = []
    for n, sums in enumerate([far, *grad(*SUM_TURNS[1:])]):
        got.append(swapped(sums, SUM_TURNS[n]))
    got.extend(grad(*SELF))
    solved = plain(
        solve_kernel, sds(Q, PT), (*got, point_inv), est=cost(2 * Q * Q * PT, Q * Q * PT * 4)
    )
    partial = ()
    for n, turn in enumerate(SELF + SOLVED_TURNS):
        piece = swapped(solved, turn) if n else solved
        partial = (
            plain(
                functools.partial(rhs_kernel, turn),
                sds(CP, FR),
                (pid, fid, res, jac, jac_cam, *partial, piece),
                est=cost(2 * 256 * 256 * 2048, 2 * 32 * 2048 * 4),
            ),
        )
    (partial,) = partial
    parts = [partial]
    for turn in CAMERA_TURNS:
        parts.append(swapped(partial, turn))

    rhs, z = plain(
        start_kernel, [sds(CP, FR), sds(8, FR)], (*parts, precond, edge), est=cost(20000, 100000)
    )
    z_left, z_right = beside(z)
    w, u = plain(
        first_kernel,
        [sds(CP, FR), sds(8, FR)],
        (z, z_left, z_right, bands, precond),
        est=cost(2 * 127 * 36 * 256, 127 * 36 * 256 * 4),
    )
    u_right = lax.ppermute(u, "frames", [(i + 1, i) for i in range(count - 1)])
    back = plain(
        back_kernel,
        [sds(2 * Q, PT)] * GROUPS,
        (pid, fid, jac, jac_cam, z, u),
        est=cost(2 * 400 * 256 * 8192, 2 * 32 * 8192 * 4),
    )
    returned = [back[GROUPS - 1]]
    for s in (3, 2, 1):
        returned.append(swapped(back[GROUPS - 1 - s], (s, s)))
    gram = plain(
        second_kernel,
        sds(count, 128),
        (u, u_right, bands, rhs, z, w),
        est=cost(127 * 36 * 256, 127 * 18 * 256 * 4),
    )
    gram = lax.all_to_all(gram, "frames", split_axis=0, concat_axis=0, tiled=True)
    undo_z, undo_u = plain(
        undo_kernel,
        [sds(Q, PT)] * 2,
        (*returned, point_inv),
        raw=(4,),
        scratch=[pltpu.VMEM((Q, Q, PT), F32), pltpu.SemaphoreType.DMA],
        est=cost(4 * Q * Q * PT, Q * Q * PT * 4),
    )
    camera_step, point_step = plain(
        final_kernel,
        [sds(CP, FR), sds(Q, PT)],
        (gram, z, u, solved, undo_z, undo_u),
        est=cost(6 * Q * PT, 6 * Q * PT * 4),
    )
    return camera_step, point_step


def solution(mesh):
    placed = (
        P(("frames", "points")),
        P(("frames", "points")),
        P(("frames", "points")),
        P(None, None, ("frames", "points")),
        P(None, None, ("frames", "points")),
        P(None, ("frames", "points")),
        P(None, None, ("frames", "points")),
        P(None, None, None, "frames"),
        P("frames"),
        P(None, None, "frames"),
    )
    return jax.shard_map(
        step,
        mesh=mesh,
        in_specs=placed,
        out_specs=(P(None, "frames"), P(None, ("frames", "points"))),
        check_vma=False,
    )
```

```python
import functools

import jax
import jax.numpy as jnp
from jax import lax
from jax.experimental import pallas as pl
from jax.experimental.pallas import tpu as pltpu
from jax.sharding import PartitionSpec as P


F32 = jnp.float32
BF16 = jnp.bfloat16
CP = 6
Q = 24
BANDW = 127
REACH = 63
FR = 256
PT = 1024
CAP = 2048
GROUPS = 4
LO = 256
HI = PT // LO
SUM_TURNS = ((2, 2), (1, 3), (3, 1))
SOLVED_TURNS = ((3, 1), (1, 3), (2, 2))
CAMERA_TURNS = ((3, 1), (2, 2), (1, 3))
BACK_TURNS = ((3, 1), (2, 2), (1, 3), (0, 0))
SELF = ((0, 0),)
LIMIT = pltpu.CompilerParams(vmem_limit_bytes=12 * 2**20)


def halves(x):
    lead = x.astype(BF16).astype(F32)
    return jnp.concatenate([lead, x - lead], axis=0).astype(BF16)


def one_hot(row, rows):
    n = row.shape[1]
    index = lax.broadcasted_iota(jnp.int32, (rows, 128), 0).astype(F32).astype(BF16)
    row = row.astype(BF16)
    cols = []
    for c in range(n // 128):
        here = jnp.broadcast_to(row[:, c * 128 : (c + 1) * 128], (rows, 128))
        cols.append(jnp.where(index == here, jnp.ones_like(index), jnp.zeros_like(index)))
    return jnp.concatenate(cols, axis=1)


def split_ids(ids):
    hi = lax.shift_right_logical(ids, 8)
    lo = lax.bitwise_and(ids, LO - 1)
    return hi.astype(F32), lo.astype(F32)


def used_or(ids, count, other):
    lane = lax.broadcasted_iota(jnp.int32, ids.shape, 1)
    return jnp.where(lane < count, ids, other)


def scatter_points(terms, ids):
    n = terms.shape[0]
    hi, lo = split_ids(ids)
    parts = halves(terms)
    table = one_hot(lo, LO)
    rows = []
    for h in range(HI):
        mask = jnp.broadcast_to((hi == h).astype(F32), (2 * n, CAP)).astype(BF16)
        rows.append(parts * mask)
    sums = lax.dot_general(
        jnp.concatenate(rows, axis=0), table, (((1,), (1,)), ((), ())), preferred_element_type=F32
    )
    out = []
    for h in range(HI):
        block = sums[h * 2 * n : (h + 1) * 2 * n]
        out.append(block[:n] + block[n:])
    return jnp.concatenate(out, axis=1)


def gather_points(values, ids):
    n = values.shape[0]
    hi, lo = split_ids(ids)
    parts = halves(values)
    table = one_hot(lo, LO)
    stacked = jnp.concatenate([parts[:, h * LO : (h + 1) * LO] for h in range(HI)], axis=0)
    got = lax.dot_general(stacked, table, (((1,), (0,)), ((), ())), preferred_element_type=F32)
    total = None
    for h in range(HI):
        block = got[h * 2 * n : (h + 1) * 2 * n]
        term = (block[:n] + block[n:]) * (hi == h).astype(F32)
        total = term if total is None else total + term
    return total


def block_at(turn):
    first = lax.rem(lax.axis_index("frames"), 2) == 0
    return lax.bitwise_xor(lax.axis_index("points"), jnp.where(first, turn[0], turn[1]))


def lanes(b):
    return pl.ds(pl.multiple_of(b * CAP, CAP), CAP)


def fetch(pairs, sems):
    copies = [pltpu.make_async_copy(src, dst, sems.at[i]) for i, (src, dst) in enumerate(pairs)]
    for copy in copies:
        copy.start()
    return copies


def sums_toward(b, ids_ref, res_ref, jp_ref):
    at = lanes(b)
    terms = jp_ref[0, :, at] * res_ref[0:1, at] + jp_ref[1, :, at] * res_ref[1:2, at]
    return scatter_points(terms, ids_ref[:, at])


def load_kernel(
    count_hbm, pid_hbm, fid_hbm, res_hbm, jp_hbm, out_ref, pid_ref, fid_ref, res_ref, jp_ref, count_ref, sems
):
    small = [(count_hbm, count_ref), (pid_hbm, pid_ref), (res_hbm, res_ref), (fid_hbm, fid_ref)]
    blocks = [block_at(turn) for turn in SUM_TURNS + SELF]
    large = [(jp_hbm.at[:, :, lanes(b)], jp_ref.at[:, :, lanes(b)]) for b in blocks]
    copies = fetch(small[:3] + large[:1] + small[3:] + large[1:], sems)
    for copy in copies[:3]:
        copy.wait()
    for g in range(GROUPS):
        here = slice(g * CAP, (g + 1) * CAP)
        pid_ref[:, here] = used_or(pid_ref[:, here], count_ref[g], PT)
    copies[3].wait()
    out_ref[...] = sums_toward(blocks[0], pid_ref, res_ref, jp_ref)
    copies[4].wait()
    for g in range(GROUPS):
        here = slice(g * CAP, (g + 1) * CAP)
        fid_ref[:, here] = used_or(fid_ref[:, here], count_ref[g], FR)
    for copy in copies[5:]:
        copy.wait()


def grad_kernel(turns, ids_ref, res_ref, jp_ref, *outs):
    for turn, out_ref in zip(turns, outs):
        out_ref[...] = sums_toward(block_at(turn), ids_ref, res_ref, jp_ref)


def solve_kernel(a_ref, b_ref, c_ref, d_ref, inv_ref, out_ref):
    grad = a_ref[...] + b_ref[...] + c_ref[...] + d_ref[...]
    out_ref[...] = jnp.sum(inv_ref[...] * grad[None], axis=1)


def rhs_kernel(turn, pid_ref, fid_ref, res_ref, jp_ref, jc_ref, *rest):
    solved_ref, out_ref = rest[-2:]
    b = block_at(turn)
    at = lanes(b)
    seen = gather_points(solved_ref[...], pid_ref[:, at])
    remain = [
        res_ref[a : a + 1, at] - jnp.sum(jp_ref[a, :, at] * seen, axis=0, keepdims=True)
        for a in range(2)
    ]
    cam = jc_ref[0, :, at] * remain[0] + jc_ref[1, :, at] * remain[1]
    cam = jnp.concatenate([cam, jnp.zeros((2, CAP), F32)], axis=0)
    table = one_hot(fid_ref[:, at].astype(F32), FR)
    sums = lax.dot_general(
        halves(cam), table, (((1,), (1,)), ((), ())), preferred_element_type=F32
    )
    total = sums[0:CP] + sums[8 : 8 + CP]
    out_ref[...] = total if len(rest) == 2 else total + rest[0][...]


def apply_precond(pre_ref, vec):
    return jnp.sum(pre_ref[...] * vec[None], axis=1)


def start_kernel(a_ref, b_ref, c_ref, d_ref, pre_ref, edge_ref, r_ref, z_ref):
    rhs = a_ref[...] + b_ref[...] + c_ref[...] + d_ref[...]
    r_ref[...] = rhs
    lane = lax.broadcasted_iota(jnp.int32, (1, FR), 1)
    last = lax.axis_index("frames") == lax.axis_size("frames") - 1
    edge = edge_ref[...] * jnp.where((lane == FR - 1) & last, 0.0, 1.0)
    z = apply_precond(pre_ref, rhs)
    z_ref[...] = jnp.concatenate([z, edge, jnp.zeros((1, FR), F32)], axis=0)


def steps_of(row):
    n = row.shape[1]
    sub = lax.broadcasted_iota(jnp.int32, (8, n), 0)
    x = jnp.broadcast_to(row, (8, n))
    for bit in (1, 2, 4):
        x = jnp.where((sub & bit) != 0, pltpu.roll(x, n - bit, 1), x)
    return x


def banded_sums(band_ref, rows, tiles, first=None):
    totals = [None] * CP
    ends = [None] * CP
    for j in range(CP):
        stepped = steps_of(rows[j])
        for t in tiles:
            at = 128 - REACH + 8 * t
            shifted = stepped[:, at : at + FR]
            if t == first:
                sub = lax.broadcasted_iota(jnp.int32, (8, FR), 0)
                shifted = jnp.where(sub == 7, 0.5 * shifted, 0.0)
            for i in range(CP):
                if 8 * t + 8 <= BANDW:
                    term = band_ref[i, j, 8 * t : 8 * t + 8, :] * shifted
                    totals[i] = term if totals[i] is None else totals[i] + term
                else:
                    count = BANDW - 8 * t
                    term = band_ref[i, j, 8 * t : BANDW, :] * shifted[:count]
                    ends[i] = term if ends[i] is None else ends[i] + term
    return jnp.concatenate(
        [
            jnp.sum(t, axis=0, keepdims=True) + jnp.sum(e, axis=0, keepdims=True)
            for t, e in zip(totals, ends)
        ],
        axis=0,
    )


def first_kernel(z_ref, outer_ref, inner_ref, band_ref, pre_ref, w_ref, u_ref):
    even = lax.rem(lax.axis_index("frames"), 2) == 0
    sides = (outer_ref[...], inner_ref[...])
    left = jnp.where(even, sides[0], sides[1])
    right = jnp.where(even, sides[1], sides[0])
    padded = jnp.concatenate([left, z_ref[...], right], axis=1)
    near = padded[:, FR - 128 : 2 * FR + 128]
    banded = banded_sums(band_ref, [near[j : j + 1] for j in range(CP)], range(16))
    own = z_ref[:CP, :]
    here = z_ref[CP : CP + 1, :]
    prev = padded[CP : CP + 1, FR - 1 : 2 * FR - 1]
    before = padded[:CP, FR - 1 : 2 * FR - 1]
    after = padded[:CP, FR + 1 : 2 * FR + 1]
    image = banded + prev * (own - before) + here * (own - after)
    w_ref[...] = image
    u = apply_precond(pre_ref, image)
    u_ref[...] = jnp.concatenate([u, jnp.zeros((2, FR), F32)], axis=0)


def second_kernel(u_ref, right_ref, band_ref, r_ref, z_ref, w_ref, out_ref):
    ahead = jnp.concatenate([u_ref[...], right_ref[...]], axis=1)
    near = jnp.concatenate([jnp.zeros((8, 128), F32), ahead[:, : FR + 128]], axis=1)
    upper = banded_sums(band_ref, [near[j : j + 1] for j in range(CP)], range(7, 16), first=7)
    u, z, w, r = u_ref[:CP, :], z_ref[:CP, :], w_ref[...], r_ref[...]
    edge = z_ref[CP : CP + 1, :]
    step = u - ahead[:CP, 1 : FR + 1]
    lane = lax.broadcasted_iota(jnp.int32, (1, 128), 1)
    row = jnp.zeros((1, 128), F32)
    for at, term in enumerate((r * z, z * w, w * u, 2.0 * u * upper + edge * step * step)):
        total = jnp.sum(jnp.sum(term, axis=0, keepdims=True), axis=1, keepdims=True)
        row = row + jnp.where(lane == at, total, 0.0)
    out_ref[...] = jnp.broadcast_to(row, out_ref.shape)


def back_kernel(pid_ref, fid_ref, jp_ref, jc_ref, z_ref, u_ref, *outs):
    parts = halves(jnp.concatenate([z_ref[...], u_ref[...]], axis=0))
    for j in range(GROUPS):
        b = block_at(BACK_TURNS[j])
        at = lanes(b)
        table = one_hot(fid_ref[:, at].astype(F32), FR)
        got = lax.dot_general(parts, table, (((1,), (0,)), ((), ())), preferred_element_type=F32)
        got = got[:16] + got[16:]
        terms = []
        for v in range(2):
            seen = got[v * 8 : v * 8 + CP]
            pair = [jnp.sum(jc_ref[a, :, at] * seen, axis=0, keepdims=True) for a in range(2)]
            terms.append(jp_ref[0, :, at] * pair[0] + jp_ref[1, :, at] * pair[1])
        outs[j][...] = scatter_points(jnp.concatenate(terms, axis=0), pid_ref[:, at])


def undo_kernel(a_ref, b_ref, c_ref, d_ref, inv_hbm, z_ref, u_ref, inv_ref, sem):
    pltpu.async_copy(inv_hbm, inv_ref, sem).wait()
    both = a_ref[...] + b_ref[...] + c_ref[...] + d_ref[...]
    z_ref[...] = jnp.sum(inv_ref[...] * both[None, :Q], axis=1)
    u_ref[...] = jnp.sum(inv_ref[...] * both[None, Q:], axis=1)


def final_kernel(g_ref, z_ref, u_ref, ps_ref, pz_ref, pu_ref, cam_ref, pt_ref):
    row = jnp.sum(g_ref[...], axis=0, keepdims=True)
    rz, zw, wu, uy = [row[:, i : i + 1] for i in range(4)]
    a0 = rz / zw
    inner = a0 * a0 * wu - rz
    beta = 1.0 + inner / rz
    curve = beta * beta * zw - 2.0 * beta * a0 * wu + a0 * a0 * uy
    a1 = inner / curve
    c0 = a0 + a1 * beta
    c1 = -a1 * a0
    cam_ref[...] = c0 * z_ref[:CP, :] + c1 * u_ref[:CP, :]
    pt_ref[...] = ps_ref[...] - c0 * pz_ref[...] - c1 * pu_ref[...]


def swapped(value, turn):
    pairs = [
        (GROUPS * f + p, GROUPS * f + (p ^ turn[f % 2]))
        for f in range(lax.axis_size("frames"))
        for p in range(GROUPS)
    ]
    return lax.ppermute(value, ("frames", "points"), pairs)


def beside(value):
    count = lax.axis_size("frames")
    inner = [(i, i ^ 1) for i in range(count)]
    outer = [pair for i in range(1, count - 1, 2) for pair in ((i, i + 1), (i + 1, i))]
    far = lax.ppermute(value, "frames", outer)
    near = lax.ppermute(value, "frames", inner)
    return far, near


def sds(*shape):
    return jax.ShapeDtypeStruct(shape, F32)


def cost(flops, moved):
    return pl.CostEstimate(flops=flops, bytes_accessed=moved, transcendentals=0)


def plain(kernel, outs, args, smem=(), raw=(), scratch=(), est=None, ):
    space = lambda i: pltpu.SMEM if i in smem else pltpu.HBM if i in raw else pltpu.VMEM
    specs = [pl.BlockSpec(memory_space=space(i)) for i in range(len(args))]
    args = [pltpu.with_memory_space_constraint(x, pltpu.HBM) if i in raw else x for i, x in enumerate(args)]
    out_specs = jax.tree.map(lambda _: pl.BlockSpec(memory_space=pltpu.VMEM), outs)
    return pl.pallas_call(
        kernel,
        in_specs=specs,
        out_specs=out_specs,
        out_shape=outs,
        scratch_shapes=list(scratch),
        cost_estimate=est,
        compiler_params=LIMIT,
    )(*args)


def step(
    obs_count,
    obs_point,
    obs_frame,
    jac_cam,
    jac_point,
    residual,
    point_inv,
    band,
    edge_weight,
    precond,
):
    slots = obs_point.shape[0]
    pid = obs_point.reshape(1, slots)
    fid = obs_frame.reshape(1, slots)
    count = lax.axis_size("frames")
    edge = edge_weight.reshape(1, FR)
    bands = jnp.transpose(band, (1, 2, 0, 3))

    ints = jax.ShapeDtypeStruct((1, slots), jnp.int32)
    far, pid, fid, res, jac = plain(
        load_kernel,
        [sds(Q, PT), ints, ints, sds(2, slots), sds(2, Q, slots)],
        (obs_count, pid, fid, residual, jac_point),
        raw=(0, 1, 2, 3, 4),
        scratch=[pltpu.SMEM((GROUPS,), jnp.int32), pltpu.SemaphoreType.DMA((8,))],
        est=cost(2 * 192 * 256 * 2048, 2 * 24 * 8192 * 4),
    )
    grad = lambda *turns: plain(
        functools.partial(grad_kernel, turns),
        [sds(Q, PT)] * len(turns),
        (pid, res, jac),
        est=cost(2 * 192 * 256 * 2048 * len(turns), 2 * 24 * 2048 * 4 * len(turns)),
    )
    got = []
    for n, sums in enumerate([far, *grad(*SUM_TURNS[1:])]):
        got.append(swapped(sums, SUM_TURNS[n]))
    got.extend(grad(*SELF))
    solved = plain(
        solve_kernel, sds(Q, PT), (*got, point_inv), est=cost(2 * Q * Q * PT, Q * Q * PT * 4)
    )
    partial = ()
    for n, turn in enumerate(SELF + SOLVED_TURNS):
        piece = swapped(solved, turn) if n else solved
        partial = (
            plain(
                functools.partial(rhs_kernel, turn),
                sds(CP, FR),
                (pid, fid, res, jac, jac_cam, *partial, piece),
                est=cost(2 * 256 * 256 * 2048, 2 * 32 * 2048 * 4),
            ),
        )
    (partial,) = partial
    parts = [partial]
    for turn in CAMERA_TURNS:
        parts.append(swapped(partial, turn))

    rhs, z = plain(
        start_kernel, [sds(CP, FR), sds(8, FR)], (*parts, precond, edge), est=cost(20000, 100000)
    )
    z_left, z_right = beside(z)
    w, u = plain(
        first_kernel,
        [sds(CP, FR), sds(8, FR)],
        (z, z_left, z_right, bands, precond),
        est=cost(2 * 127 * 36 * 256, 127 * 36 * 256 * 4),
    )
    u_right = lax.ppermute(u, "frames", [(i + 1, i) for i in range(count - 1)])
    back = plain(
        back_kernel,
        [sds(2 * Q, PT)] * GROUPS,
        (pid, fid, jac, jac_cam, z, u),
        est=cost(2 * 400 * 256 * 8192, 2 * 32 * 8192 * 4),
    )
    returned = [back[GROUPS - 1]]
    for s in (3, 2, 1):
        returned.append(swapped(back[GROUPS - 1 - s], BACK_TURNS[GROUPS - 1 - s]))
    gram = plain(
        second_kernel,
        sds(count, 128),
        (u, u_right, bands, rhs, z, w),
        est=cost(127 * 36 * 256, 127 * 18 * 256 * 4),
    )
    gram = lax.all_to_all(gram, "frames", split_axis=0, concat_axis=0, tiled=True)
    undo_z, undo_u = plain(
        undo_kernel,
        [sds(Q, PT)] * 2,
        (*returned, point_inv),
        raw=(4,),
        scratch=[pltpu.VMEM((Q, Q, PT), F32), pltpu.SemaphoreType.DMA],
        est=cost(4 * Q * Q * PT, Q * Q * PT * 4),
    )
    camera_step, point_step = plain(
        final_kernel,
        [sds(CP, FR), sds(Q, PT)],
        (gram, z, u, solved, undo_z, undo_u),
        est=cost(6 * Q * PT, 6 * Q * PT * 4),
    )
    return camera_step, point_step


def solution(mesh):
    placed = (
        P(("frames", "points")),
        P(("frames", "points")),
        P(("frames", "points")),
        P(None, None, ("frames", "points")),
        P(None, None, ("frames", "points")),
        P(None, ("frames", "points")),
        P(None, None, ("frames", "points")),
        P(None, None, None, "frames"),
        P("frames"),
        P(None, None, "frames"),
    )
    return jax.shard_map(
        step,
        mesh=mesh,
        in_specs=placed,
        out_specs=(P(None, "frames"), P(None, ("frames", "points"))),
        check_vma=False,
    )
```
